32 devices in a mesh: sec: 2 (over core), grp: 4 (over y, x), dev: 4 (over z).
Axes of the slice: x: 2, y: 2, z: 4, core: 2. Of those that a mesh axis runs over, the one named last changes fastest.
Arguments:
- current: float32 [32, 196608], P(None, ('sec', 'grp', 'dev')), may hold values from -6 to 6
- prior: float32 [8, 32, 196608], P(None, None, ('sec', 'grp', 'dev')), as said below
- block_values: float32 [1024, 6, 9216], P(('grp', 'dev')), may hold values from -0.25 to 0.25
- block_cols: int32 [1024, 6], P(('grp', 'dev')), may hold values from 0 to 63
- face_match: int32 [16, 4, 1536], P(('grp', 'dev')), may hold values from 0 to 1535, each once within a row
- face_weight: float32 [16, 4, 1536], P(('grp', 'dev')), may hold values from -3 to 3
- fluid_diag: float32 [98304], P(('grp', 'dev')), may hold values from 2 to 4
- wet_source: int32 [49152], P(('grp', 'dev')), may hold values from 0 to 6143
- wet_dest: int32 [49152, 1], P(('grp', 'dev')), may hold values from 0 to 15; in each aligned block of 3072 rows (0 to 3071, 3072 to 6143, ...) at most 392 rows name the same one
- wet_target: int32 [49152], P(('grp', 'dev')), may hold values from 0 to 6143
- wet_weight: float32 [49152], P(('grp', 'dev')), may hold values from -5 to 5
Outputs:
- next_block: float32 [32, 196608], P(None, ('sec', 'grp', 'dev'))
- coeffs: float32 [8, 32, 32], replicated
- rfac: float32 [32, 32], replicated
The draws below stay inside these ranges and needn't reach their ends.
Inputs may be any that keep to these rules, and one draw needn't show every extreme that they name: `block_cols`: block columns index blocks within the same subdomain. `face_match`: each subdomain's matching of one round is a permutation of its face. `prior`: each earlier block's columns have about unit length. `wet_dest`: among one structure subdomain's couplings, at most 392 name the same fluid subdomain, and some subdomain has exactly 392 for one.
All inputs are finite; a program needn't handle non-finite values.
Results may differ from the reference program's by a relative error of at most 0.00008.
Values sent between devices are 32-bit elements; how exact they have to be, the bound alone decides.
A program may use at most 128 MiB of HBM per device.

```python
import math
import jax
import jax.numpy as jnp
import numpy as np
from jax import lax

K = 32
NPRIOR = 8
BS = 96
RB = 64
NB = 6
ROUNDS = 4
R = 6144
FACE = 1536
WS = 3072
P_SIZE = 16
CAP = 392
ROWS = 196608
N_GRP = 4
N_DEV = 4


def draw_prior(key, part):
    first_key = jax.random.fold_in(key, 11)
    second_key = jax.random.fold_in(key, 12)
    fresh = jax.random.truncated_normal(first_key, -4.0, 4.0, (NPRIOR, K, ROWS), jnp.float32)
    shared = jax.random.truncated_normal(second_key, -4.0, 4.0, (1, K, ROWS), jnp.float32)
    return (fresh + 0.5 * shared) * (1.0 / math.sqrt(1.25 * ROWS))


def plant(entries, key, least, top_value):
    shape = entries.shape
    spot = [jax.random.randint(jax.random.fold_in(key, axis), (), 0, shape[axis]) for axis in range(len(shape))]
    entries = entries.at[tuple(spot)].set(least)
    longest = shape.index(max(shape))
    spot[longest] = (spot[longest] + 1) % shape[longest]
    return entries.at[tuple(spot)].set(top_value)


def steps_of(rng, shape, shards, least, largest):
    loudness = 1.0
    for axis_at, shards_of in shards:
        steps = jax.random.uniform(jax.random.fold_in(jax.random.fold_in(rng, 6), axis_at), (shards_of,), jnp.float32, least / len(shards), largest / len(shards))
        loudness = loudness * jnp.repeat(jnp.exp(steps), shape[axis_at] // shards_of).reshape((-1,) + (1,) * (len(shape) - 1 - axis_at))
    return loudness


def shared_out(key, own, number, rows, amount, top, limit, lean):
    order = jax.random.permutation(key, amount)
    crowded, common = shares(amount, rows * top, limit, lean, True), shares(amount, rows * top, limit, lean, False)
    places = jnp.arange(amount)

    def named(sizes, offset_by):
        used = int((sizes > 0).sum())
        fixed = max(1, used // 4)
        passed = fixed + (places - fixed + offset_by * (used - fixed)) % max(1, amount - fixed)
        return jnp.zeros((amount,), jnp.int32).at[order[jnp.where(places < fixed, places, passed)]].set(jnp.asarray(sizes, jnp.int32))

    sizes = jnp.where(number % 4 == 0, named(crowded, number // 4), named(common, number - number // 4 - 1))
    mixed = jax.random.permutation(jax.random.fold_in(own, 3), amount)
    giver, taker = mixed[0:amount // 2 * 2:2], mixed[1:amount // 2 * 2:2]
    margin = jnp.minimum(sizes[giver] - 1, limit - sizes[taker]) // 2
    margin = jnp.where((giver == order[0]) | (taker == order[0]) | (sizes[taker] == 0), 0, jnp.maximum(margin, 0))
    passed = jax.random.randint(jax.random.fold_in(own, 4), (amount // 2,), 0, 1 << 20) % (margin + 1)
    sizes = sizes.at[giver].add(-passed).at[taker].add(passed)
    labels = jnp.searchsorted(jnp.cumsum(sizes), jnp.arange(rows * top), side="right").astype(jnp.int32)
    table = labels.reshape(top, rows).T
    table = table[jax.random.permutation(jax.random.fold_in(own, 1), rows)]
    offset_by = jax.random.randint(jax.random.fold_in(own, 2), (rows, 1), 0, top)
    return jnp.take_along_axis(table, (jnp.arange(top)[None, :] + offset_by) % top, axis=1)


def shares(amount, total, limit, skew, full):
    weights = [(1 << 20) // math.isqrt(standing ** skew) + 1 for standing in range(1, amount + 1)]
    largest = limit if full else min(limit, max(-(-total // amount), total * weights[0] // sum(weights)))
    least = 1 if total - largest >= amount - 1 else 0
    given, rest = [largest] + [least] * (amount - 1), total - largest - least * (amount - 1)
    while rest > 0:
        movable = [i for i in range(1, amount) if given[i] < largest] or [i for i in range(1, amount) if given[i] < limit]
        pool, left = sum([weights[i] for i in movable]), rest
        for i in movable:
            addition = min(limit - given[i], max(1, left * weights[i] // pool), rest)
            given[i] = given[i] + addition
            rest = rest - addition
    return np.array(given)


def normal_values(key, extent, scale, reach, pieces=(), held_as=jnp.bfloat16):
    entries = scale * jax.random.normal(key, extent, jnp.float32)
    if pieces:
        entries = entries * steps_of(key, extent, pieces, -0.22, 0.18)
    return jnp.clip(entries, -reach, reach).astype(held_as)


def setup_inputs(seed: int = 0) -> dict:
    splits = jax.random.split(jax.random.key(seed), 12)
    current = normal_values(splits[0], (K, ROWS), 1.0, 6.0, ((1, 32),), jnp.float32)
    prior = draw_prior(jax.random.fold_in(splits[11], 71), 0)
    block_values = normal_values(splits[2], (P_SIZE * RB, NB, BS * BS), (BS * NB) ** -0.5, 0.25, ((0, 16),), jnp.float32)
    block_cols = plant(jax.random.randint(splits[3], (P_SIZE * RB, NB), 0, RB), jax.random.fold_in(splits[3], 1), 0, RB - 1).astype(jnp.int32)
    face_match = jax.vmap(lambda own: jax.random.permutation(own, FACE))(jax.random.split(splits[4], P_SIZE * ROUNDS)).reshape((P_SIZE, ROUNDS, FACE)).astype(jnp.int32)
    face_weight = normal_values(splits[5], (P_SIZE, ROUNDS, FACE), 0.5, 3.0, ((0, 16),), jnp.float32)
    fluid_diag = jnp.clip(2.0 + 2.0 * jax.random.uniform(splits[6], (P_SIZE * R,), jnp.float32) ** steps_of(splits[6], (P_SIZE * R,), ((0, 16),), -0.2, 0.2), 2.0, 4.0)
    wet_source = plant(jax.random.randint(splits[7], (P_SIZE * WS,), 0, R), jax.random.fold_in(splits[7], 1), 0, R - 1).astype(jnp.int32)
    wet_dest_keys = jax.random.split(jax.random.fold_in(splits[8], 1), (P_SIZE * WS) // WS)
    wet_dest_turns = jax.random.permutation(jax.random.fold_in(splits[8], 3), (P_SIZE * WS) // WS)
    wet_dest = jax.vmap(lambda own, number: shared_out(jax.random.fold_in(splits[8], 2), own, number, WS, P_SIZE, 1, CAP, 2))(wet_dest_keys, wet_dest_turns).reshape((P_SIZE * WS, 1))
    wet_target = plant(jax.random.randint(splits[9], (P_SIZE * WS,), 0, R), jax.random.fold_in(splits[9], 1), 0, R - 1).astype(jnp.int32)
    wet_weight = normal_values(splits[10], (P_SIZE * WS,), 1.0, 5.0, ((0, 16),), jnp.float32)
    return {"current": current, "prior": prior, "block_values": block_values, "block_cols": block_cols, "face_match": face_match, "face_weight": face_weight, "fluid_diag": fluid_diag, "wet_source": wet_source, "wet_dest": wet_dest, "wet_target": wet_target, "wet_weight": wet_weight}


def reference(current, prior, block_values, block_cols, face_match, face_weight, fluid_diag, wet_source, wet_dest, wet_target, wet_weight):
    highest = lax.Precision.HIGHEST
    subdomains = N_GRP * N_DEV
    local_rows = BS * RB
    half_rows = subdomains * local_rows
    structure = current[:, :half_rows].reshape(K, subdomains, local_rows)
    fluid_half = current[:, half_rows:]
    values = block_values.reshape(subdomains, RB, NB, BS, BS)
    columns = block_cols.reshape(subdomains, RB, NB)

    def apply_one(packed):
        block_vals, block_idx, local_vec = packed
        picked = local_vec.reshape(K, RB, BS)[:, block_idx, :]
        return jnp.einsum('kibc,ibrc->kir', picked, block_vals, precision=highest).reshape(K, local_rows)
    shell = lax.map(apply_one, (values, columns, jnp.moveaxis(structure, 1, 0)))
    shell = jnp.moveaxis(shell, 0, 1)
    flips = [1, 2, N_DEV, 2 * N_DEV]
    owners = jnp.arange(subdomains, dtype=jnp.int32)
    for sweep in range(ROUNDS):
        partner = owners ^ flips[sweep]
        faces = structure[:, :, sweep * FACE:(sweep + 1) * FACE][:, partner, :]
        matched = jnp.take_along_axis(faces, face_match[None, :, sweep, :], axis=2)
        shell = shell.at[:, :, sweep * FACE:(sweep + 1) * FACE].add(face_weight[None, :, sweep, :] * matched)
    zero_col = jnp.zeros((K, 1), jnp.float32)
    before = jnp.concatenate([zero_col, fluid_half[:, :-1]], axis=1)
    after = jnp.concatenate([fluid_half[:, 1:], zero_col], axis=1)
    fluid_out = fluid_diag[None, :] * fluid_half - before - after
    couple_owner = jnp.arange(subdomains * WS, dtype=jnp.int32) // WS
    source_cols = couple_owner * local_rows + wet_source
    target_cols = wet_dest[:, 0] * local_rows + wet_target
    moved = wet_weight[None, :] * structure.reshape(K, half_rows)[:, source_cols]
    fluid_flat = fluid_out.at[:, target_cols].add(moved)
    image = jnp.concatenate([shell.reshape(K, half_rows), fluid_flat], axis=1)
    h_first = jnp.einsum('jkr,lr->jkl', prior, image, precision=highest)
    w_one = image - jnp.einsum('jkl,jkr->lr', h_first, prior, precision=highest)
    h_second = jnp.einsum('jkr,lr->jkl', prior, w_one, precision=highest)
    w_two = w_one - jnp.einsum('jkl,jkr->lr', h_second, prior, precision=highest)
    gram = jnp.dot(w_two, w_two.T, precision=highest) / ROWS
    factor = jnp.linalg.cholesky(gram)
    next_block = lax.linalg.triangular_solve(factor, w_two, left_side=True, lower=True)
    return (next_block, h_first + h_second, factor.T)
```

```python
import functools

import jax
import jax.numpy as jnp
from jax import lax
from jax.experimental import pallas as pl
from jax.experimental.pallas import tpu as pltpu
from jax.sharding import PartitionSpec as P

BS = 96
NB = 6
ROUNDS = 4
LANES = 128
META = 8
PART = 32
F32 = jnp.float32
BF16 = jnp.bfloat16
NT = (((1,), (1,)), ((), ()))
ALL = ("sec", "grp", "dev")


def split2(x):
    hi = x.astype(BF16)
    return hi, (x - hi.astype(F32)).astype(BF16)


def nt(a, b):
    return lax.dot_general(a, b, NT, preferred_element_type=F32)


def lane_gather(x, low):
    return jnp.take_along_axis(x, low, axis=1)


def wet_sort(subdomains, per, src_ref, dest_ref, tgt_ref, w_ref, meta_ref):
    blocks = src_ref.shape[0]
    slabs = subdomains * per
    dest = dest_ref[...]
    lane = lax.broadcasted_iota(jnp.int32, (LANES, LANES), 1)
    sub = lax.broadcasted_iota(jnp.int32, (LANES, LANES), 0)
    tri = jnp.where(sub < lane, 1.0, 0.0).astype(BF16)
    ones = jnp.ones((LANES, LANES), BF16)
    low_tri = jnp.where(
        lax.broadcasted_iota(jnp.int32, (blocks, blocks), 1)
        < lax.broadcasted_iota(jnp.int32, (blocks, blocks), 0),
        1.0,
        0.0,
    ).astype(BF16)

    def count(q, rank):
        mine = dest == q
        oh = jnp.where(mine, 1.0, 0.0).astype(BF16)
        within = jnp.dot(oh, tri, preferred_element_type=F32)
        totals = jnp.dot(oh, ones, preferred_element_type=F32).astype(BF16)
        offset = jnp.dot(low_tri, totals, preferred_element_type=F32)
        return jnp.where(mine, within + offset, rank)

    rank = lax.fori_loop(0, subdomains, count, jnp.zeros(dest.shape, F32)).astype(jnp.int32)
    slab = dest * per + rank // LANES
    spot = rank % LANES
    src = src_ref[...]
    tgt = tgt_ref[...]
    w = w_ref[...]
    w0 = w.astype(BF16).astype(F32)
    w1 = (w - w0).astype(BF16).astype(F32)
    w2 = w - w0 - w1
    fields = [src // LANES, src % LANES, tgt // LANES, tgt % LANES]
    fields = [f.astype(F32) for f in fields] + [w0, w1, w2]
    acc = jnp.zeros((len(fields) * slabs, LANES), F32)
    slab_row = lax.broadcasted_iota(jnp.int32, (slabs, LANES), 0)
    for i in range(blocks):
        hit = slab_row == slab[i : i + 1, :]
        lhs = jnp.concatenate([jnp.where(hit, f[i : i + 1, :], 0.0) for f in fields], axis=0)
        oh = jnp.where(sub == spot[i : i + 1, :], 1.0, 0.0)
        acc = acc + nt(lhs.astype(BF16), oh.astype(BF16))
    parts = [acc[f * slabs : (f + 1) * slabs] for f in range(len(fields))]
    meta_ref[0] = parts[0]
    meta_ref[1] = parts[1]
    meta_ref[2] = parts[2] * LANES + parts[3]
    meta_ref[3] = parts[4] + parts[5] + parts[6]


class Wet:
    def __init__(self, subdomains, per, mine, x_ref, meta_ref, pack_ref, got_ref, lhs_ref, acc_ref, sems):
        self.subdomains, self.per, self.mine, self.x_ref, self.meta_ref = subdomains, per, mine, x_ref, meta_ref
        self.pack_ref, self.got_ref, self.lhs_ref, self.acc_ref, self.sems = pack_ref, got_ref, lhs_ref, acc_ref, sems
        self.width, self.rows = x_ref.shape

    def gather(self, a, ref, to):
        width, row = self.width, pl.ds(a, 1)
        high = jnp.broadcast_to(self.meta_ref[0, row, :].astype(jnp.int32), (width, LANES))
        low = jnp.broadcast_to(self.meta_ref[1, row, :].astype(jnp.int32), (width, LANES))
        got = jnp.zeros((width, LANES), F32)
        for h in range(self.rows // LANES):
            piece = lane_gather(self.x_ref[:, h * LANES : (h + 1) * LANES], low)
            got = jnp.where(high == h, piece, got)
        ref[to, :width, :] = got * self.meta_ref[3, row, :]
        ref[to, width:, :] = jnp.broadcast_to(self.meta_ref[2, row, :], (META, LANES))

    def copy(self, to, at):
        per = self.per
        return remote(
            self.pack_ref.at[pl.ds(to * per, per)], self.got_ref.at[pl.ds(at * per, per)], self.sems.at[0, to],
            self.sems.at[1, at], place(self.subdomains + to),
        )

    def send(self, first, last):
        per, mine = self.per, self.mine

        def body(s, carry):
            q = lax.rem(mine + s, self.subdomains)

            def one(p, inner):
                self.gather(q * per + p, self.pack_ref, q * per + p)
                return inner

            lax.fori_loop(0, per, one, 0)
            self.copy(q, mine).start()
            return carry

        lax.fori_loop(first, last, body, 0)

    def keep(self):
        def one(p, inner):
            self.gather(self.mine * self.per + p, self.got_ref, self.mine * self.per + p)
            return inner

        lax.fori_loop(0, self.per, one, 0)

    def add(self, q):
        width, wide = self.width, 2 * LANES
        highs = self.rows // wide
        got_ref, lhs_ref = self.got_ref, self.lhs_ref
        ohs = []
        for s in range(self.per):
            a = q * self.per + s
            target = got_ref[a, width : width + 1, :].astype(jnp.int32)
            vals = got_ref[a, :width, :]
            hi = vals.astype(BF16).astype(F32)
            lo = vals - hi
            high = jnp.broadcast_to(target // wide, (width, LANES))
            low = target % wide
            at = s * wide
            for h in range(highs):
                hit = high == h
                band = slice(h * width, (h + 1) * width)
                lhs_ref[band, at : at + LANES] = jnp.where(hit, hi, 0.0).astype(BF16)
                lhs_ref[band, at + LANES : at + wide] = jnp.where(hit, lo, 0.0).astype(BF16)
            oh = jnp.where(
                lax.broadcasted_iota(jnp.int32, (wide, LANES), 0) == low, 1.0, 0.0
            ).astype(BF16)
            ohs += [oh, oh]
        self.acc_ref[...] += nt(lhs_ref[...], jnp.concatenate(ohs, axis=1))

    def receive(self):
        subdomains, mine = self.subdomains, self.mine
        self.acc_ref[...] = jnp.zeros_like(self.acc_ref)
        self.add(mine)

        def take(s, carry):
            q = lax.rem(mine + subdomains - s, subdomains)
            self.copy(q, q).wait_recv()
            self.add(q)
            return carry

        lax.fori_loop(1, subdomains, take, 0)

    def drain(self):
        def body(s, carry):
            self.copy(lax.rem(self.mine + s, self.subdomains), self.mine).wait_send()
            return carry

        lax.fori_loop(1, self.subdomains, body, 0)


def fluid_image(mine, subdomains, own_ref, diag_ref, edge_ref, acc_ref, image_ref):
    width, rows = own_ref.shape
    edges = [
        jnp.where(mine == 0, 0.0, edge_ref[0]),
        jnp.where(mine == subdomains - 1, 0.0, edge_ref[1]),
    ]
    lane = lax.broadcasted_iota(jnp.int32, (width, LANES), 1)
    pieces = rows // LANES
    for t in range(pieces):
        own = own_ref[:, t * LANES : (t + 1) * LANES]
        prev = edges[0] if t == 0 else own_ref[:, (t - 1) * LANES : t * LANES]
        nxt = edges[1] if t == pieces - 1 else own_ref[:, (t + 1) * LANES : (t + 2) * LANES]
        before = jnp.where(lane == 0, pltpu.roll(prev, 1, 1), pltpu.roll(own, 1, 1))
        after = jnp.where(
            lane == LANES - 1, pltpu.roll(nxt, LANES - 1, 1), pltpu.roll(own, LANES - 1, 1)
        )
        h, side = t // 2, t % 2
        added = acc_ref[h * width : (h + 1) * width, side * LANES : (side + 1) * LANES]
        d = diag_ref[:, t * LANES : (t + 1) * LANES]
        image_ref[:, t * LANES : (t + 1) * LANES] = d * own - before - after + added


def stack_terms(hi, lo):
    zero = jnp.zeros_like(hi)
    return jnp.concatenate([hi, lo, zero, zero, zero, zero, hi, lo], axis=0)


def shell_prepare(x_ref, left_ref, right_ref):
    lanes = lax.broadcasted_iota(jnp.int32, (LANES, LANES), 1)
    subs = lax.broadcasted_iota(jnp.int32, (LANES, LANES), 0)
    eye = jnp.where(lanes == subs, 1.0, 0.0).astype(BF16)

    def body(t, carry):
        at = pl.ds(pl.multiple_of(t * LANES, LANES), LANES)
        v = x_ref[:, at]
        hi = v.astype(BF16).astype(F32)
        both = nt(eye, stack_terms(hi, v - hi).astype(BF16)).astype(BF16)
        to = pl.ds(t * (LANES // PART), LANES // PART)
        left_ref[to] = both[:, :LANES].reshape(LANES // PART, PART, LANES)
        right_ref[to] = both[:, LANES:].reshape(LANES // PART, PART, LANES)
        return carry

    lax.fori_loop(0, x_ref.shape[1] // LANES, body, 0)


def shell_rows(group, cols_ref, blocks_ref, left_ref, right_ref, even_ref, odd_ref):
    chunks = BS * BS // LANES
    high = chunks // 3
    lane = lax.broadcasted_iota(jnp.int32, (high, LANES), 1)
    first = lane % (LANES // 2) < LANES // 4
    front = lane < LANES // 2
    for r in range(8):
        row = group * 8 + r
        at = [cols_ref[row, b] * (BS // PART) for b in range(NB)]
        outs = []
        for s in range(3):
            v = jnp.concatenate(
                [
                    blocks_ref[b, pl.ds(group * chunks * 8 + 8 * s + r, high, stride=24), :]
                    for b in range(NB)
                ],
                axis=1,
            )
            hi = v.astype(BF16).astype(F32)
            lhs = jnp.concatenate([hi, v - hi], axis=0).astype(BF16)
            spans = (
                ((left_ref, 0), (left_ref, 1), (left_ref, 2), (right_ref, 0)),
                ((right_ref, 1), (right_ref, 2), (left_ref, 0), (left_ref, 1)),
                ((left_ref, 2), (right_ref, 0), (right_ref, 1), (right_ref, 2)),
            )[s]
            rhs = jnp.concatenate([ref[at[b] + o] for b in range(NB) for ref, o in spans], axis=0)
            outs.append(jnp.dot(lhs, rhs, preferred_element_type=F32))

        def fold(z):
            return z[:high] + jnp.where(first, z[high:], 0.0)

        u = [fold(z) for z in outs]
        to = pl.ds(pl.multiple_of(row * high, 8), high)
        even_ref[to, :] = u[0] + jnp.where(front, 0.0, u[1])
        odd_ref[to, :] = u[2] + jnp.where(front, u[1], 0.0)


def shell_store(even_ref, odd_ref, out_ref):
    width = out_ref.shape[0]
    lane = lax.broadcasted_iota(jnp.int32, (width, LANES), 1)
    phase = lane % 4

    def body(t, carry):
        at = pl.ds(pl.multiple_of(t * LANES, LANES), LANES)
        even, odd = even_ref[at, :].T, odd_ref[at, :].T
        y = [
            even[:width] + even[width : 2 * width],
            even[2 * width : 3 * width] + even[3 * width :],
            odd[:width] + odd[width : 2 * width],
            odd[2 * width : 3 * width] + odd[3 * width :],
        ]
        for o in range(4):
            index = lane // 4 + 32 * o
            g = [lane_gather(v, index) for v in y]
            got = jnp.where(phase == 0, g[0], jnp.where(phase == 1, g[1], jnp.where(phase == 2, g[2], g[3])))
            out_ref[:, pl.ds(pl.multiple_of(t * 4 * LANES, LANES) + o * LANES, LANES)] = got
        return carry

    lax.fori_loop(0, even_ref.shape[0] // LANES, body, 0)


def add_faces(faces_ref, match_ref, weight_ref, out_ref):
    width = out_ref.shape[0]
    rounds, face = match_ref.shape
    pieces = face // LANES
    for m in range(rounds):
        for o in range(pieces):
            index = match_ref[m : m + 1, o * LANES : (o + 1) * LANES]
            high = jnp.broadcast_to(index // LANES, (width, LANES))
            low = jnp.broadcast_to(index % LANES, (width, LANES))
            got = jnp.zeros((width, LANES), F32)
            for h in range(pieces):
                piece = lane_gather(faces_ref[m, :, h * LANES : (h + 1) * LANES], low)
                got = jnp.where(high == h, piece, got)
            at = m * face + o * LANES
            w = weight_ref[m : m + 1, o * LANES : (o + 1) * LANES]
            out_ref[:, at : at + LANES] += w * got


MESH = pl.DeviceIdType.MESH


def place(index):
    dev = lax.axis_size("dev")
    grp = lax.axis_size("grp")
    return (index // (grp * dev), index // dev % grp, index % dev)


def turns(axis):
    count = lax.axis_size(axis)
    ring = [lax.axis_index(axis)]
    for _ in range(1, count):
        following = ring[-1] + 1
        ring.append(jnp.where(following == count, 0, following))
    return ring


def announce():
    barrier = pltpu.get_barrier_semaphore()
    rings = [turns(axis) for axis in ALL]
    for i, s in enumerate(rings[0]):
        for j, g in enumerate(rings[1]):
            for k, d in enumerate(rings[2]):
                if i or j or k:
                    pl.semaphore_signal(barrier, inc=1, device_id=(s, g, d), device_id_type=MESH)
    return barrier


def remote(src, dst, send, recv, device):
    return pltpu.make_async_remote_copy(
        src_ref=src, dst_ref=dst, send_sem=send, recv_sem=recv, device_id=device,
        device_id_type=MESH,
    )


class Reduce:
    def __init__(self, stage, slots, along, total, sems):
        self.stage, self.slots, self.along, self.total, self.sems = stage, slots, along, total, sems
        self.sec, self.g, self.d = (lax.axis_index(axis) for axis in ALL)
        self.grp = lax.axis_size("grp")
        self.me = self.sec * self.grp + self.g

    def plane(self, body):
        for i, s in enumerate(turns("sec")):
            for j, g in enumerate(turns("grp")):
                if i or j:
                    body(s * self.grp + g, (s, g, self.d))

    def bulk(self, source, target, first):
        rest = pl.ds(0, source.shape[0] - 1)
        other = (1 - self.sec, self.g, self.d)
        return remote(source.at[rest], target.at[rest], self.sems.at[first], self.sems.at[first + 1], other)

    def scatter(self):
        self.plane(
            lambda p, where: remote(
                self.stage.at[p], self.slots.at[self.me], self.sems.at[0], self.sems.at[1], where
            ).start()
        )

    def middle(self):
        self.bulk(self.stage, self.slots, 0).wait_recv()
        self.slots[self.me] = self.stage[self.me]
        self.along[self.d] = jnp.sum(self.slots[...], axis=0)
        for d in turns("dev")[1:]:
            remote(
                self.along.at[self.d], self.along.at[self.d], self.sems.at[2], self.sems.at[3],
                (self.sec, self.g, d),
            ).start()

    def gather(self):
        self.bulk(self.along, self.along, 2).wait_recv()
        self.total[self.me] = jnp.sum(self.along[...], axis=0)
        self.plane(
            lambda p, where: remote(
                self.total.at[self.me], self.total.at[self.me], self.sems.at[4], self.sems.at[5], where
            ).start()
        )

    def finish(self):
        self.bulk(self.total, self.total, 4).wait_recv()

    def drain(self):
        self.bulk(self.stage, self.slots, 0).wait_send()
        self.bulk(self.along, self.along, 2).wait_send()
        self.bulk(self.total, self.total, 4).wait_send()


def step_kernel(names, subdomains, per, total_rows, *refs):
    r = dict(zip(names, refs))
    n = 2 * subdomains
    sec, g, d = (lax.axis_index(axis) for axis in ALL)
    mine = g * lax.axis_size("dev") + d
    x_ref, image_ref = r["x"], r["image"]
    width, rows = x_ref.shape
    face = r["match"].shape[1]
    held, high_ref, low_ref = r["held"], r["high"], r["low"]
    basis = held.shape[0]
    chunk = rows // r["held_sems"].shape[0]
    groups = r["block_sems"].shape[0]

    def local(name, i):
        return pltpu.make_async_copy(r[name + "_hbm"], r[name], r["local_sems"].at[i])

    def prior_copy(i):
        at = pl.ds(pl.multiple_of(i * chunk, chunk), chunk)
        return pltpu.make_async_copy(r["prior_hbm"].at[:, at], held.at[:, at], r["held_sems"].at[i])

    def block_copy(i):
        span = r["blocks"].shape[1] // groups
        at = pl.ds(pl.multiple_of(i * span, 8), span)
        return pltpu.make_async_copy(r["blocks_hbm"].at[:, at], r["blocks"].at[:, at], r["block_sems"].at[i])

    structure = ("match", "weight")
    fluid = ("src", "dest", "tgt", "w", "diag")
    local("x", 0).start()

    @pl.when(sec == 1)
    def _():
        for i, name in enumerate(fluid):
            local(name, 1 + i).start()

    for i in range(rows // chunk):
        prior_copy(i).start()

    @pl.when(sec == 0)
    def _():
        for i in range(groups):
            block_copy(i).start()
        for i, name in enumerate(structure):
            local(name, 1 + i).start()

    barrier = announce()
    local("x", 0).wait()

    @pl.when(sec == 0)
    def _():
        shell_prepare(x_ref, r["left"], r["right"])

    @pl.when(sec == 1)
    def _():
        for i, name in enumerate(fluid):
            local(name, 1 + i).wait()
        wet_sort(subdomains, per, r["src"], r["dest"], r["tgt"], r["w"], r["meta"])

    pl.semaphore_wait(barrier, n - 1)
    partners = [
        (0, g, d + 1 - 2 * lax.rem(d, 2)),
        (0, g, d + 2 - 4 * lax.rem(d // 2, 2)),
        (0, g + 1 - 2 * lax.rem(g, 2), d),
        (0, g + 2 - 4 * lax.rem(g // 2, 2), d),
    ]

    def face_copy(m):
        return remote(
            x_ref.at[:, pl.ds(m * face, face)], r["faces"].at[m], r["face_sems"].at[0, m],
            r["face_sems"].at[1, m], partners[m],
        )

    def edge_copy(side):
        to = subdomains + lax.rem(mine + (1 if side == 0 else subdomains - 1), subdomains)
        at = rows - LANES if side == 0 else 0
        return remote(
            x_ref.at[:, pl.ds(at, LANES)], r["edge"].at[side], r["edge_sems"].at[0, side],
            r["edge_sems"].at[1, side], place(to),
        )

    def twin_copy():
        return remote(x_ref, r["xs"], r["twin_sems"].at[0], r["twin_sems"].at[1], (1, g, d))

    @pl.when(sec == 0)
    def _():
        twin_copy().start()
        for m in range(ROUNDS):
            face_copy(m).start()

    @pl.when(sec == 1)
    def _():
        edge_copy(0).start()
        edge_copy(1).start()

    def product(i, carry):
        same, mixed = carry
        prior_copy(i).wait()
        at = pl.ds(pl.multiple_of(i * chunk, chunk), chunk)
        hi, lo = split2(held[:, at])
        high_ref[:, at] = hi
        low_ref[:, at] = lo
        return same + nt(hi, hi), mixed + nt(hi, lo)

    zero = jnp.zeros((basis, basis), F32)
    same, mixed = lax.fori_loop(0, rows // chunk, product, (zero, zero))
    part = same + mixed + mixed.T
    cross_sum = Reduce(r["g_stage"], r["g_slots"], r["g_along"], r["g_total"], r["g_sems"])
    cross_sum.stage[...] = part.reshape(cross_sum.stage.shape)
    cross_sum.scatter()
    wet = Wet(
        subdomains, per, mine, r["xs"], r["meta"], r["pack"], r["got"], r["lhs"], r["acc"], r["wet_sems"]
    )

    def shell(first, last):
        def body(i, carry):
            block_copy(i).wait()
            shell_rows(i, r["cols"], r["blocks"], r["left"], r["right"], r["even"], r["odd"])
            return carry

        lax.fori_loop(first, last, body, 0)

    @pl.when(sec == 0)
    def _():
        shell(0, groups // 2)

    @pl.when(sec == 1)
    def _():
        twin_copy().wait_recv()
        wet.send(1, subdomains // 2)

    cross_sum.middle()

    @pl.when(sec == 0)
    def _():
        shell(groups // 2, groups)

    @pl.when(sec == 1)
    def _():
        wet.send(subdomains // 2, subdomains)
        wet.keep()

    cross_sum.gather()

    @pl.when(sec == 0)
    def _():
        shell_store(r["even"], r["odd"], image_ref)
        for i, name in enumerate(structure):
            local(name, 1 + i).wait()
        for m in range(ROUNDS):
            face_copy(m).wait()
        add_faces(r["faces"], r["match"], r["weight"], image_ref)
        twin_copy().wait_send()

    @pl.when(sec == 1)
    def _():
        wet.receive()
        edge_copy(0).wait()
        edge_copy(1).wait()
        fluid_image(mine, subdomains, x_ref, r["diag"], r["edge"], r["acc"], image_ref)
        wet.drain()

    ih, il = split2(image_ref[...])
    both = nt(jnp.concatenate([ih, il], axis=0), high_ref[...])
    head = both[:width] + both[width:] + nt(ih, low_ref[...])
    mixed = nt(ih, il)
    square = nt(ih, ih) + mixed + mixed.T
    part = jnp.concatenate(
        [head, square, jnp.zeros((width, -(basis + width) % LANES), F32)], axis=1
    )
    head_sum = Reduce(r["h_stage"], r["h_slots"], r["h_along"], r["h_total"], r["h_sems"])
    count, piece = head_sum.stage.shape[:2]
    for i in range(count):
        head_sum.stage[i] = part[i * piece : (i + 1) * piece]
    head_sum.scatter()
    cross_sum.finish()
    cross_sum.drain()
    head_sum.middle()
    head_sum.gather()
    head_sum.finish()
    head_sum.drain()
    cross = cross_sum.total[...].reshape(basis, basis)
    summed = jnp.concatenate([head_sum.total[i] for i in range(count)], axis=0)
    first = summed[:, :basis]
    square = summed[:, basis : basis + width]
    highest = lax.Precision.HIGHEST

    def dot(a, b):
        return jnp.dot(a, b, precision=highest, preferred_element_type=F32)

    def dot_nt(a, b):
        return lax.dot_general(a, b, NT, precision=highest, preferred_element_type=F32)

    coef = 2.0 * first - dot(first, cross)
    gram = (
        square - dot_nt(coef, first) - dot_nt(first, coef) + dot_nt(dot(coef, cross), coef)
    ) * (1.0 / total_rows)
    r["coef"][...] = coef.T
    sub = lax.broadcasted_iota(jnp.int32, (width, 2 * width), 0)
    lane = lax.broadcasted_iota(jnp.int32, (width, 2 * width), 1)
    eye = jnp.where(sub + width == lane, 1.0, 0.0)
    work = jnp.concatenate([gram, jnp.zeros((width, width), F32)], axis=1) + eye
    for j in range(width):
        root = jnp.sqrt(work[j : j + 1, j : j + 1])
        row = work[j : j + 1, :] / root
        column = work[:, j : j + 1] / root
        work = jnp.where(sub == j, row, jnp.where(sub > j, work - column * row, work))
    r["fac"][...] = jnp.where(sub <= lane, work, 0.0)[:, :width]
    inverse = work[:, width:]
    mix = -dot(inverse, coef)
    vh, vl = split2(inverse)
    mh, ml = split2(mix)
    vs = jnp.concatenate([vh, vl], axis=0)
    ms = jnp.concatenate([mh, ml], axis=0)

    def out(i, carry):
        at = pl.ds(pl.multiple_of(i * chunk, chunk), chunk)
        ih, il = split2(image_ref[:, at])
        a = jnp.dot(ms, high_ref[:, at], preferred_element_type=F32)
        a = a + jnp.dot(vs, ih, preferred_element_type=F32)
        c = jnp.dot(mh, low_ref[:, at], preferred_element_type=F32)
        c = c + jnp.dot(vh, il, preferred_element_type=F32)
        r["next"][:, at] = a[:width] + a[width:] + c
        return carry

    lax.fori_loop(0, rows // chunk, out, 0)


def shards(
    current, prior, block_values, block_cols, face_match, face_weight,
    fluid_diag, wet_source, wet_dest, wet_target, wet_weight,
):
    width, local_rows = current.shape
    face_rows = face_match.shape[2]
    row_blocks = block_cols.shape[0]
    wet_slots = wet_source.shape[0]
    grp, dev = lax.axis_size("grp"), lax.axis_size("dev")
    subdomains = grp * dev
    total_rows = local_rows * lax.axis_size("sec") * subdomains
    capacity = 2 * wet_slots // subdomains + 8
    per = -(-capacity // LANES)
    slabs = subdomains * per
    flat_prior = prior.reshape(-1, local_rows)
    basis = flat_prior.shape[0]
    plane = 2 * grp
    group = row_blocks // 8
    tiles = block_values.transpose(1, 0, 2).reshape(NB, group, 8, BS * BS // LANES, LANES)
    tiles = tiles.transpose(0, 1, 3, 2, 4).reshape(NB, row_blocks * BS * BS // LANES, LANES)
    tiled = (wet_slots // LANES, LANES)
    any_spec, smem = pl.BlockSpec(memory_space=pl.ANY), pl.BlockSpec(memory_space=pltpu.SMEM)
    spec = pl.BlockSpec(memory_space=pltpu.VMEM)
    inputs = {
        "x_hbm": current, "prior_hbm": flat_prior, "blocks_hbm": tiles, "cols": block_cols,
        "match_hbm": face_match[0], "weight_hbm": face_weight[0], "diag_hbm": fluid_diag[None, :],
        "src_hbm": wet_source.reshape(tiled), "dest_hbm": wet_dest.reshape(tiled),
        "tgt_hbm": wet_target.reshape(tiled), "w_hbm": wet_weight.reshape(tiled),
    }
    outputs = {
        "next": jax.ShapeDtypeStruct((width, local_rows), F32),
        "coef": jax.ShapeDtypeStruct((basis, width), F32),
        "fac": jax.ShapeDtypeStruct((width, width), F32),
    }
    lanes = -(-(basis + width) // LANES) * LANES
    slab = pltpu.VMEM((slabs, width + META, LANES), F32)
    bands = local_rows // (2 * LANES) * width
    field = pltpu.VMEM((width, local_rows), F32)
    cross_piece = pltpu.VMEM((plane, basis // plane, basis), F32)
    head_piece = pltpu.VMEM((plane, width // plane, lanes), F32)
    dma = pltpu.SemaphoreType.DMA
    scratch = {
        "image": field, "x": field, "xs": field,
        "held": pltpu.VMEM((basis, local_rows), F32),
        "high": pltpu.VMEM((basis, local_rows), BF16), "low": pltpu.VMEM((basis, local_rows), BF16),
        "blocks": pltpu.VMEM(tiles.shape, F32),
        "left": pltpu.VMEM((local_rows // PART, PART, LANES), BF16),
        "right": pltpu.VMEM((local_rows // PART, PART, LANES), BF16),
        "even": pltpu.VMEM((local_rows // 4, LANES), F32), "odd": pltpu.VMEM((local_rows // 4, LANES), F32),
        "faces": pltpu.VMEM((ROUNDS, width, face_rows), F32),
        "edge": pltpu.VMEM((2, width, LANES), F32),
        "match": pltpu.VMEM((ROUNDS, face_rows), jnp.int32), "weight": pltpu.VMEM((ROUNDS, face_rows), F32),
        "diag": pltpu.VMEM((1, local_rows), F32),
        "src": pltpu.VMEM(tiled, jnp.int32), "dest": pltpu.VMEM(tiled, jnp.int32),
        "tgt": pltpu.VMEM(tiled, jnp.int32), "w": pltpu.VMEM(tiled, F32),
        "meta": pltpu.VMEM((4, slabs, LANES), F32),
        "pack": slab, "got": slab,
        "lhs": pltpu.VMEM((bands, 2 * per * LANES), BF16), "acc": pltpu.VMEM((bands, 2 * LANES), F32),
        "g_stage": cross_piece, "g_slots": cross_piece, "g_total": cross_piece,
        "g_along": pltpu.VMEM((dev, basis // plane, basis), F32),
        "h_stage": head_piece, "h_slots": head_piece, "h_total": head_piece,
        "h_along": pltpu.VMEM((dev, width // plane, lanes), F32),
        "local_sems": dma((6,)), "held_sems": dma((local_rows // 1024,)), "block_sems": dma((group,)),
        "face_sems": dma((2, ROUNDS)), "edge_sems": dma((2, 2)), "twin_sems": dma((2,)),
        "wet_sems": dma((2, subdomains)), "g_sems": dma((6,)), "h_sems": dma((6,)),
    }
    names = (*inputs, *outputs, *scratch)
    next_block, coef, factor = pl.pallas_call(
        functools.partial(step_kernel, names, subdomains, per, total_rows),
        out_shape=tuple(outputs.values()),
        in_specs=[smem if name == "cols" else any_spec for name in inputs],
        out_specs=(spec,) * len(outputs),
        scratch_shapes=list(scratch.values()),
        compiler_params=pltpu.CompilerParams(
            vmem_limit_bytes=60 << 20, collective_id=0, has_side_effects=True
        ),
    )(*inputs.values())
    return (next_block, coef.reshape(prior.shape[0], width, width), factor)


def solution(mesh):
    placed = (
        P(None, ALL),
        P(None, None, ALL),
        P(("grp", "dev"), None, None),
        P(("grp", "dev"), None),
        P(("grp", "dev"), None, None),
        P(("grp", "dev"), None, None),
        P(("grp", "dev")),
        P(("grp", "dev")),
        P(("grp", "dev"), None),
        P(("grp", "dev")),
        P(("grp", "dev")),
    )
    return jax.shard_map(
        shards, mesh=mesh, in_specs=placed, out_specs=(P(None, ALL), P(), P()), check_vma=False
    )
```

```python
import functools

import jax
import jax.numpy as jnp
from jax import lax
from jax.experimental import pallas as pl
from jax.experimental.pallas import tpu as pltpu
from jax.sharding import PartitionSpec as P

BS = 96
NB = 6
ROUNDS = 4
LANES = 128
QUAD = 4
PART = 32
F32 = jnp.float32
BF16 = jnp.bfloat16
NT = (((1,), (1,)), ((), ()))
ALL = ("sec", "grp", "dev")


def split2(x):
    hi = x.astype(BF16)
    return hi, (x - hi.astype(F32)).astype(BF16)


def nt(a, b):
    return lax.dot_general(a, b, NT, preferred_element_type=F32)


def lane_gather(x, low):
    return jnp.take_along_axis(x, low, axis=1)


def wet_sort(subdomains, limit, src_ref, dest_ref, tgt_ref, w_ref, index_ref, pack_ref):
    blocks = src_ref.shape[0]
    slabs = subdomains * QUAD
    top = pack_ref.shape[1] - 2 * QUAD
    dest = dest_ref[...]
    lane = lax.broadcasted_iota(jnp.int32, (LANES, LANES), 1)
    sub = lax.broadcasted_iota(jnp.int32, (LANES, LANES), 0)
    tri = jnp.where(sub < lane, 1.0, 0.0).astype(BF16)
    ones = jnp.ones((LANES, LANES), BF16)
    low_tri = jnp.where(
        lax.broadcasted_iota(jnp.int32, (blocks, blocks), 1)
        < lax.broadcasted_iota(jnp.int32, (blocks, blocks), 0),
        1.0,
        0.0,
    ).astype(BF16)

    def count(q, rank):
        mine = dest == q
        oh = jnp.where(mine, 1.0, 0.0).astype(BF16)
        within = jnp.dot(oh, tri, preferred_element_type=F32)
        totals = jnp.dot(oh, ones, preferred_element_type=F32).astype(BF16)
        offset = jnp.dot(low_tri, totals, preferred_element_type=F32)
        return jnp.where(mine, within + offset, rank)

    rank = lax.fori_loop(0, subdomains, count, jnp.zeros(dest.shape, F32)).astype(jnp.int32)
    slab = dest * QUAD + rank % QUAD
    spot = rank // QUAD
    src = src_ref[...]
    tgt = tgt_ref[...]
    w = w_ref[...]
    w0 = w.astype(BF16).astype(F32)
    w1 = (w - w0).astype(BF16).astype(F32)
    w2 = w - w0 - w1
    fields = [src // LANES, src % LANES, tgt // LANES, tgt % LANES]
    fields = [f.astype(F32) for f in fields] + [w0, w1, w2]
    acc = jnp.zeros((len(fields) * slabs, LANES), F32)
    slab_row = lax.broadcasted_iota(jnp.int32, (slabs, LANES), 0)
    for i in range(blocks):
        hit = slab_row == slab[i : i + 1, :]
        lhs = jnp.concatenate([jnp.where(hit, f[i : i + 1, :], 0.0) for f in fields], axis=0)
        oh = jnp.where(sub == spot[i : i + 1, :], 1.0, 0.0)
        acc = acc + nt(lhs.astype(BF16), oh.astype(BF16))
    parts = [acc[f * slabs : (f + 1) * slabs] for f in range(len(fields))]
    index = (parts[0] * LANES + parts[1]).astype(jnp.int32)
    index_ref[...] = jnp.minimum(jnp.maximum(index, 0), limit - 1)
    target = parts[2] * LANES + parts[3]
    weight = parts[4] + parts[5] + parts[6]
    for q in range(subdomains):
        pack_ref[q, top - 8 : top] = jnp.zeros((8, LANES), F32)
        pack_ref[q, top : top + QUAD] = target[q * QUAD : (q + 1) * QUAD]
        pack_ref[q, top + QUAD :] = weight[q * QUAD : (q + 1) * QUAD]


class Wet:
    def __init__(self, subdomains, used, mine, x_ref, rows_ref, index_ref, pack_ref, got_ref, acc_ref, sems):
        self.used = used
        self.subdomains, self.mine, self.x_ref, self.rows_ref = subdomains, mine, x_ref, rows_ref
        self.index_ref, self.pack_ref, self.got_ref, self.acc_ref, self.sems = index_ref, pack_ref, got_ref, acc_ref, sems
        self.width, self.rows = x_ref.shape
        self.top = pack_ref.shape[1] - 2 * QUAD

    def prepare(self):
        lanes = lax.broadcasted_iota(jnp.int32, (LANES, 2 * LANES), 1)
        subs = lax.broadcasted_iota(jnp.int32, (LANES, 2 * LANES), 0)
        eyes = jnp.where(lanes % LANES == subs, 1.0, 0.0).astype(BF16)

        def body(t, carry):
            at = pl.ds(pl.multiple_of(t * LANES, LANES), LANES)
            hi, lo = split2(self.x_ref[:, at])
            both = jnp.concatenate([hi, lo], axis=1)
            self.rows_ref[at, :] = nt(eyes, jnp.concatenate([both] * QUAD, axis=0))
            return carry

        lax.fori_loop(0, self.rows // LANES, body, 0, unroll=4)

    def gather(self, q):
        lane = lax.broadcasted_iota(jnp.int32, (1, LANES), 1)
        masks = [lane < LANES * (g + 1) // QUAD for g in range(QUAD - 1)]
        for row in range(self.used):
            line = [self.rows_ref[self.index_ref[q * QUAD + g, row]][None, :] for g in range(QUAD)]
            got = line[-1]
            for g in reversed(range(QUAD - 1)):
                got = jnp.where(masks[g], line[g], got)
            self.pack_ref[q, row : row + 1, :] = got

    def copy(self, to, at):
        return remote(
            self.pack_ref.at[to], self.got_ref.at[at], self.sems.at[0, to],
            self.sems.at[1, at], place(self.subdomains + to),
        )

    def send(self, first, last):
        def body(s, carry):
            q = lax.rem(self.mine + s, self.subdomains)
            self.gather(q)

            @pl.when(s < self.subdomains)
            def _():
                self.copy(q, self.mine).start()

            return carry

        lax.fori_loop(first, last, body, 0)

    def add(self, sources, first):
        width, wide, top = self.width, 2 * LANES, self.top
        highs = self.rows // wide
        pad = jnp.zeros((LANES - top - 2 * QUAD, LANES), F32)
        subs = lax.broadcasted_iota(jnp.int32, (wide, LANES), 0).astype(F32).astype(BF16)
        one, zero = jnp.ones((wide, LANES), BF16), jnp.zeros((wide, LANES), BF16)
        none = jnp.zeros((width, LANES), BF16)
        terms, high, ohs = [], [], []
        for ref, q in sources:
            turned = jnp.concatenate([ref[q], pad], axis=0).T
            for g in range(QUAD):
                target = ref[q, top + g : top + g + 1].astype(jnp.int32)
                vals = turned[g * width : (g + 1) * width] * ref[q, top + QUAD + g : top + QUAD + g + 1]
                terms.append(split2(vals))
                high.append(jnp.broadcast_to((target // wide).astype(F32), (width, LANES)).astype(BF16))
                low = jnp.broadcast_to((target % wide).astype(F32), (wide, LANES)).astype(BF16)
                oh = jnp.where(subs == low, one, zero)
                ohs += [oh, oh]
        bands = []
        for h in range(highs):
            level = jnp.full((width, LANES), h, F32).astype(BF16)
            bands.append(
                jnp.concatenate([jnp.where(up == level, t, none) for up, two in zip(high, terms) for t in two], axis=1)
            )
        more = nt(jnp.concatenate(bands, axis=0), jnp.concatenate(ohs, axis=1))
        if first:
            self.acc_ref[...] = more
        else:
            self.acc_ref[...] += more

    def receive(self, first, last):
        subdomains, mine = self.subdomains, self.mine

        def arrived(s):
            q = lax.rem(mine + subdomains - s, subdomains)
            self.copy(q, q).wait_recv()
            return self.got_ref, q

        def take(s, carry):
            self.add([arrived(2 * s), arrived(2 * s + 1)], False)
            return carry

        if first == 0:
            self.add([(self.pack_ref, mine), arrived(1)], True)
        lax.fori_loop(max(first, 1), last, take, 0)

    def drain(self):
        def body(s, carry):
            self.copy(lax.rem(self.mine + s, self.subdomains), self.mine).wait_send()
            return carry

        lax.fori_loop(1, self.subdomains, body, 0)


def fluid_image(mine, subdomains, own_ref, diag_ref, edge_ref, acc_ref, image_ref):
    width, rows = own_ref.shape
    edges = [
        jnp.where(mine == 0, 0.0, edge_ref[0]),
        jnp.where(mine == subdomains - 1, 0.0, edge_ref[1]),
    ]
    lane = lax.broadcasted_iota(jnp.int32, (width, LANES), 1)
    pieces = rows // LANES
    for t in range(pieces):
        own = own_ref[:, t * LANES : (t + 1) * LANES]
        prev = edges[0] if t == 0 else own_ref[:, (t - 1) * LANES : t * LANES]
        nxt = edges[1] if t == pieces - 1 else own_ref[:, (t + 1) * LANES : (t + 2) * LANES]
        before = jnp.where(lane == 0, pltpu.roll(prev, 1, 1), pltpu.roll(own, 1, 1))
        after = jnp.where(
            lane == LANES - 1, pltpu.roll(nxt, LANES - 1, 1), pltpu.roll(own, LANES - 1, 1)
        )
        h, side = t // 2, t % 2
        added = acc_ref[h * width : (h + 1) * width, side * LANES : (side + 1) * LANES]
        d = diag_ref[:, t * LANES : (t + 1) * LANES]
        image_ref[:, t * LANES : (t + 1) * LANES] = d * own - before - after + added


def stack_terms(hi, lo):
    zero = jnp.zeros_like(hi)
    return jnp.concatenate([hi, lo, zero, zero, zero, zero, hi, lo], axis=0)


def shell_prepare(x_ref, left_ref, right_ref):
    lanes = lax.broadcasted_iota(jnp.int32, (LANES, LANES), 1)
    subs = lax.broadcasted_iota(jnp.int32, (LANES, LANES), 0)
    eye = jnp.where(lanes == subs, 1.0, 0.0).astype(BF16)

    def body(t, carry):
        at = pl.ds(pl.multiple_of(t * LANES, LANES), LANES)
        v = x_ref[:, at]
        hi = v.astype(BF16).astype(F32)
        both = nt(eye, stack_terms(hi, v - hi).astype(BF16)).astype(BF16)
        to = pl.ds(t * (LANES // PART), LANES // PART)
        left_ref[to] = both[:, :LANES].reshape(LANES // PART, PART, LANES)
        right_ref[to] = both[:, LANES:].reshape(LANES // PART, PART, LANES)
        return carry

    lax.fori_loop(0, x_ref.shape[1] // LANES, body, 0, unroll=4)


def shell_rows(group, cols_ref, blocks_ref, left_ref, right_ref, even_ref, odd_ref):
    chunks = BS * BS // LANES
    high = chunks // 3
    lane = lax.broadcasted_iota(jnp.int32, (high, LANES), 1)
    first = lane % (LANES // 2) < LANES // 4
    front = lane < LANES // 2
    for r in range(8):
        row = group * 8 + r
        at = [cols_ref[b, row] * (BS // PART) for b in range(NB)]
        outs = []
        for s in range(3):
            v = jnp.concatenate(
                [
                    blocks_ref[b, pl.ds(group * chunks * 8 + 8 * s + r, high, stride=24), :]
                    for b in range(NB)
                ],
                axis=1,
            )
            hi = v.astype(BF16).astype(F32)
            lhs = jnp.concatenate([hi, v - hi], axis=0).astype(BF16)
            spans = (
                ((left_ref, 0), (left_ref, 1), (left_ref, 2), (right_ref, 0)),
                ((right_ref, 1), (right_ref, 2), (left_ref, 0), (left_ref, 1)),
                ((left_ref, 2), (right_ref, 0), (right_ref, 1), (right_ref, 2)),
            )[s]
            rhs = jnp.concatenate([ref[at[b] + o] for b in range(NB) for ref, o in spans], axis=0)
            outs.append(jnp.dot(lhs, rhs, preferred_element_type=F32))

        def fold(z):
            return z[:high] + jnp.where(first, z[high:], 0.0)

        u = [fold(z) for z in outs]
        to = pl.ds(pl.multiple_of(row * high, 8), high)
        even_ref[to, :] = u[0] + jnp.where(front, 0.0, u[1])
        odd_ref[to, :] = u[2] + jnp.where(front, u[1], 0.0)


def shell_store(even_ref, odd_ref, out_ref):
    width = out_ref.shape[0]
    lane = lax.broadcasted_iota(jnp.int32, (width, LANES), 1)
    phase = lane % 4

    def body(t, carry):
        at = pl.ds(pl.multiple_of(t * LANES, LANES), LANES)
        even, odd = even_ref[at, :].T, odd_ref[at, :].T
        y = [
            even[:width] + even[width : 2 * width],
            even[2 * width : 3 * width] + even[3 * width :],
            odd[:width] + odd[width : 2 * width],
            odd[2 * width : 3 * width] + odd[3 * width :],
        ]
        for o in range(4):
            index = lane // 4 + 32 * o
            g = [lane_gather(v, index) for v in y]
            got = jnp.where(phase == 0, g[0], jnp.where(phase == 1, g[1], jnp.where(phase == 2, g[2], g[3])))
            out_ref[:, pl.ds(pl.multiple_of(t * 4 * LANES, LANES) + o * LANES, LANES)] = got
        return carry

    lax.fori_loop(0, even_ref.shape[0] // LANES, body, 0)


def add_faces(faces_ref, match_ref, weight_ref, out_ref):
    width = out_ref.shape[0]
    rounds, face = match_ref.shape
    pieces = face // LANES
    for m in range(rounds):
        for o in range(pieces):
            index = match_ref[m : m + 1, o * LANES : (o + 1) * LANES]
            high = jnp.broadcast_to(index // LANES, (width, LANES))
            low = jnp.broadcast_to(index % LANES, (width, LANES))
            got = jnp.zeros((width, LANES), F32)
            for h in range(pieces):
                piece = lane_gather(faces_ref[m, :, h * LANES : (h + 1) * LANES], low)
                got = jnp.where(high == h, piece, got)
            at = m * face + o * LANES
            w = weight_ref[m : m + 1, o * LANES : (o + 1) * LANES]
            out_ref[:, at : at + LANES] += w * got


MESH = pl.DeviceIdType.MESH


def place(index):
    dev = lax.axis_size("dev")
    grp = lax.axis_size("grp")
    return (index // (grp * dev), index // dev % grp, index % dev)


def turns(axis):
    count = lax.axis_size(axis)
    ring = [lax.axis_index(axis)]
    for _ in range(1, count):
        following = ring[-1] + 1
        ring.append(jnp.where(following == count, 0, following))
    return ring


def announce():
    barrier = pltpu.get_barrier_semaphore()
    rings = [turns(axis) for axis in ALL]
    for i, s in enumerate(rings[0]):
        for j, g in enumerate(rings[1]):
            for k, d in enumerate(rings[2]):
                if i or j or k:
                    pl.semaphore_signal(barrier, inc=1, device_id=(s, g, d), device_id_type=MESH)
    return barrier


def remote(src, dst, send, recv, device):
    return pltpu.make_async_remote_copy(
        src_ref=src, dst_ref=dst, send_sem=send, recv_sem=recv, device_id=device,
        device_id_type=MESH,
    )


class Reduce:
    def __init__(self, stage, slots, along, total, sems):
        self.stage, self.slots, self.along, self.total, self.sems = stage, slots, along, total, sems
        self.sec, self.g, self.d = (lax.axis_index(axis) for axis in ALL)
        self.grp = lax.axis_size("grp")
        self.me = self.sec * self.grp + self.g

    def plane(self, body):
        for i, s in enumerate(turns("sec")):
            for j, g in enumerate(turns("grp")):
                if i or j:
                    body(s * self.grp + g, (s, g, self.d))

    def bulk(self, source, target, first):
        rest = pl.ds(0, source.shape[0] - 1)
        other = (1 - self.sec, self.g, self.d)
        return remote(source.at[rest], target.at[rest], self.sems.at[first], self.sems.at[first + 1], other)

    def scatter(self):
        self.plane(
            lambda p, where: remote(
                self.stage.at[p], self.slots.at[self.me], self.sems.at[0], self.sems.at[1], where
            ).start()
        )

    def middle(self):
        self.bulk(self.stage, self.slots, 0).wait_recv()
        self.slots[self.me] = self.stage[self.me]
        self.along[self.d] = jnp.sum(self.slots[...], axis=0)
        for d in turns("dev")[1:]:
            remote(
                self.along.at[self.d], self.along.at[self.d], self.sems.at[2], self.sems.at[3],
                (self.sec, self.g, d),
            ).start()

    def gather(self):
        self.bulk(self.along, self.along, 2).wait_recv()
        self.total[self.me] = jnp.sum(self.along[...], axis=0)
        self.plane(
            lambda p, where: remote(
                self.total.at[self.me], self.total.at[self.me], self.sems.at[4], self.sems.at[5], where
            ).start()
        )

    def finish(self):
        self.bulk(self.total, self.total, 4).wait_recv()

    def drain(self):
        self.bulk(self.stage, self.slots, 0).wait_send()
        self.bulk(self.along, self.along, 2).wait_send()
        self.bulk(self.total, self.total, 4).wait_send()


def step_kernel(names, subdomains, used, total_rows, *refs):
    r = dict(zip(names, refs))
    n = 2 * subdomains
    sec, g, d = (lax.axis_index(axis) for axis in ALL)
    mine = g * lax.axis_size("dev") + d
    x_ref, image_ref = r["x"], r["image"]
    width, rows = x_ref.shape
    face = r["match"].shape[1]
    held, high_ref, low_ref = r["held"], r["high"], r["low"]
    basis = held.shape[0]
    chunk = rows // r["held_sems"].shape[0]
    groups = r["block_sems"].shape[0]

    def local(name, i):
        return pltpu.make_async_copy(r[name + "_hbm"], r[name], r["local_sems"].at[i])

    def prior_copy(i):
        at = pl.ds(pl.multiple_of(i * chunk, chunk), chunk)
        return pltpu.make_async_copy(r["prior_hbm"].at[:, at], held.at[:, at], r["held_sems"].at[i])

    def block_copy(i):
        span = r["blocks"].shape[1] // groups
        at = pl.ds(pl.multiple_of(i * span, 8), span)
        return pltpu.make_async_copy(r["blocks_hbm"].at[:, at], r["blocks"].at[:, at], r["block_sems"].at[i])

    structure = ("match", "weight", "cols")
    fluid = ("src", "dest", "tgt", "w", "diag")
    local("x", 0).start()

    @pl.when(sec == 1)
    def _():
        for i, name in enumerate(fluid):
            local(name, 1 + i).start()

    for i in range(rows // chunk):
        prior_copy(i).start()

    @pl.when(sec == 0)
    def _():
        for i in range(groups):
            block_copy(i).start()
        for i, name in enumerate(structure):
            local(name, 1 + i).start()

    barrier = announce()
    index_copy = pltpu.make_async_copy(r["index"], r["index_smem"], r["local_sems"].at[6])
    local("x", 0).wait()

    @pl.when(sec == 0)
    def _():
        shell_prepare(x_ref, r["left"], r["right"])

    @pl.when(sec == 1)
    def _():
        for i, name in enumerate(fluid):
            local(name, 1 + i).wait()
        wet_sort(subdomains, rows, r["src"], r["dest"], r["tgt"], r["w"], r["index"], r["pack"])
        index_copy.start()

    pl.semaphore_wait(barrier, n - 1)
    partners = [
        (0, g, d + 1 - 2 * lax.rem(d, 2)),
        (0, g, d + 2 - 4 * lax.rem(d // 2, 2)),
        (0, g + 1 - 2 * lax.rem(g, 2), d),
        (0, g + 2 - 4 * lax.rem(g // 2, 2), d),
    ]

    def face_copy(m):
        return remote(
            x_ref.at[:, pl.ds(m * face, face)], r["faces"].at[m], r["face_sems"].at[0, m],
            r["face_sems"].at[1, m], partners[m],
        )

    def edge_copy(side):
        to = subdomains + lax.rem(mine + (1 if side == 0 else subdomains - 1), subdomains)
        at = rows - LANES if side == 0 else 0
        return remote(
            x_ref.at[:, pl.ds(at, LANES)], r["edge"].at[side], r["edge_sems"].at[0, side],
            r["edge_sems"].at[1, side], place(to),
        )

    def twin_copy():
        return remote(x_ref, r["xs"], r["twin_sems"].at[0], r["twin_sems"].at[1], (1, g, d))

    @pl.when(sec == 0)
    def _():
        twin_copy().start()
        for m in range(ROUNDS):
            face_copy(m).start()

    @pl.when(sec == 1)
    def _():
        edge_copy(0).start()
        edge_copy(1).start()

    wet = Wet(
        subdomains, used, mine, r["xs"], r["wet_rows"], r["index_smem"], r["pack"], r["got"], r["acc"], r["wet_sems"]
    )

    def shell(first, last):
        def body(i, carry):
            block_copy(i).wait()
            shell_rows(i, r["cols"], r["blocks"], r["left"], r["right"], r["even"], r["odd"])
            return carry

        lax.fori_loop(first, last, body, 0)

    @pl.when(sec == 0)
    def _():
        local("cols", 3).wait()
        shell(0, groups)

    @pl.when(sec == 1)
    def _():
        twin_copy().wait_recv()
        wet.prepare()
        index_copy.wait()
        wet.send(1, subdomains + 1)

    def product(i, carry):
        same, mixed = carry
        prior_copy(i).wait()
        at = pl.ds(pl.multiple_of(i * chunk, chunk), chunk)
        hi, lo = split2(held[:, at])
        high_ref[:, at] = hi
        low_ref[:, at] = lo
        return same + nt(hi, hi), mixed + nt(hi, lo)

    zero = jnp.zeros((basis, basis), F32)
    same, mixed = lax.fori_loop(0, rows // chunk, product, (zero, zero))
    part = same + mixed + mixed.T
    cross_sum = Reduce(r["g_stage"], r["g_slots"], r["g_along"], r["g_total"], r["g_sems"])
    cross_sum.stage[...] = part.reshape(cross_sum.stage.shape)
    cross_sum.scatter()

    @pl.when(sec == 0)
    def _():
        shell_store(r["even"], r["odd"], image_ref)

    pairs = subdomains // 2

    @pl.when(sec == 1)
    def _():
        wet.receive(0, pairs // 2)

    cross_sum.middle()

    @pl.when(sec == 0)
    def _():
        for i, name in enumerate(structure[:2]):
            local(name, 1 + i).wait()
        for m in range(ROUNDS):
            face_copy(m).wait()
        add_faces(r["faces"], r["match"], r["weight"], image_ref)
        twin_copy().wait_send()

    @pl.when(sec == 1)
    def _():
        wet.receive(pairs // 2, pairs)
        edge_copy(0).wait()
        edge_copy(1).wait()
        fluid_image(mine, subdomains, x_ref, r["diag"], r["edge"], r["acc"], image_ref)
        wet.drain()

    cross_sum.gather()
    ih, il = split2(image_ref[...])
    both = nt(jnp.concatenate([ih, il], axis=0), high_ref[...])
    head = both[:width] + both[width:] + nt(ih, low_ref[...])
    mixed = nt(ih, il)
    square = nt(ih, ih) + mixed + mixed.T
    part = jnp.concatenate(
        [head, square, jnp.zeros((width, -(basis + width) % LANES), F32)], axis=1
    )
    head_sum = Reduce(r["h_stage"], r["h_slots"], r["h_along"], r["h_total"], r["h_sems"])
    count, piece = head_sum.stage.shape[:2]
    for i in range(count):
        head_sum.stage[i] = part[i * piece : (i + 1) * piece]
    head_sum.scatter()
    cross_sum.finish()
    cross_sum.drain()
    head_sum.middle()
    head_sum.gather()
    head_sum.finish()
    head_sum.drain()
    cross = cross_sum.total[...].reshape(basis, basis)
    summed = jnp.concatenate([head_sum.total[i] for i in range(count)], axis=0)
    first = summed[:, :basis]
    square = summed[:, basis : basis + width]
    highest = lax.Precision.HIGHEST

    def dot(a, b):
        return jnp.dot(a, b, precision=highest, preferred_element_type=F32)

    def dot_nt(a, b):
        return lax.dot_general(a, b, NT, precision=highest, preferred_element_type=F32)

    coef = 2.0 * first - dot(first, cross)
    gram = (
        square - dot_nt(coef, first) - dot_nt(first, coef) + dot_nt(dot(coef, cross), coef)
    ) * (1.0 / total_rows)
    r["coef"][...] = coef.T
    sub = lax.broadcasted_iota(jnp.int32, (width, 2 * width), 0)
    lane = lax.broadcasted_iota(jnp.int32, (width, 2 * width), 1)
    eye = jnp.where(sub + width == lane, 1.0, 0.0)
    work = jnp.concatenate([gram, jnp.zeros((width, width), F32)], axis=1) + eye
    for j in range(width):
        row = work[j : j + 1, :] / work[j : j + 1, j : j + 1]
        work = jnp.where(sub > j, work - work[:, j : j + 1] * row, work)
    pivots = jnp.sum(jnp.where(sub == lane, work, 0.0), axis=1, keepdims=True)
    work = work / jnp.sqrt(pivots)
    r["fac"][...] = jnp.where(sub <= lane, work, 0.0)[:, :width]
    inverse = work[:, width:]
    mix = -dot(inverse, coef)
    vh, vl = split2(inverse)
    mh, ml = split2(mix)
    vs = jnp.concatenate([vh, vl], axis=0)
    ms = jnp.concatenate([mh, ml], axis=0)

    def out(i, carry):
        at = pl.ds(pl.multiple_of(i * chunk, chunk), chunk)
        ih, il = split2(image_ref[:, at])
        a = jnp.dot(ms, high_ref[:, at], preferred_element_type=F32)
        a = a + jnp.dot(vs, ih, preferred_element_type=F32)
        c = jnp.dot(mh, low_ref[:, at], preferred_element_type=F32)
        c = c + jnp.dot(vh, il, preferred_element_type=F32)
        r["next"][:, at] = a[:width] + a[width:] + c
        return carry

    lax.fori_loop(0, rows // chunk, out, 0)


def shards(
    current, prior, block_values, block_cols, face_match, face_weight,
    fluid_diag, wet_source, wet_dest, wet_target, wet_weight,
):
    width, local_rows = current.shape
    face_rows = face_match.shape[2]
    row_blocks = block_cols.shape[0]
    wet_slots = wet_source.shape[0]
    grp, dev = lax.axis_size("grp"), lax.axis_size("dev")
    subdomains = grp * dev
    total_rows = local_rows * lax.axis_size("sec") * subdomains
    capacity = 2 * wet_slots // subdomains + 8
    slabs = subdomains * QUAD
    used = -(-capacity // QUAD)
    slots = -(-used // 8) * 8
    flat_prior = prior.reshape(-1, local_rows)
    basis = flat_prior.shape[0]
    plane = 2 * grp
    group = row_blocks // 8
    tiles = block_values.transpose(1, 0, 2).reshape(NB, group, 8, BS * BS // LANES, LANES)
    tiles = tiles.transpose(0, 1, 3, 2, 4).reshape(NB, row_blocks * BS * BS // LANES, LANES)
    tiled = (wet_slots // LANES, LANES)
    any_spec = pl.BlockSpec(memory_space=pl.ANY)
    spec = pl.BlockSpec(memory_space=pltpu.VMEM)
    inputs = {
        "x_hbm": current, "prior_hbm": flat_prior, "blocks_hbm": tiles, "cols_hbm": block_cols.T,
        "match_hbm": face_match[0], "weight_hbm": face_weight[0], "diag_hbm": fluid_diag[None, :],
        "src_hbm": wet_source.reshape(tiled), "dest_hbm": wet_dest.reshape(tiled),
        "tgt_hbm": wet_target.reshape(tiled), "w_hbm": wet_weight.reshape(tiled),
    }
    outputs = {
        "next": jax.ShapeDtypeStruct((width, local_rows), F32),
        "coef": jax.ShapeDtypeStruct((basis, width), F32),
        "fac": jax.ShapeDtypeStruct((width, width), F32),
    }
    lanes = -(-(basis + width) // LANES) * LANES
    slab = pltpu.VMEM((subdomains, slots + 2 * QUAD, LANES), F32)
    bands = local_rows // (2 * LANES) * width
    field = pltpu.VMEM((width, local_rows), F32)
    cross_piece = pltpu.VMEM((plane, basis // plane, basis), F32)
    head_piece = pltpu.VMEM((plane, width // plane, lanes), F32)
    dma = pltpu.SemaphoreType.DMA
    scratch = {
        "cols": pltpu.SMEM((NB, row_blocks), jnp.int32),
        "image": field, "x": field, "xs": field,
        "held": pltpu.VMEM((basis, local_rows), F32),
        "high": pltpu.VMEM((basis, local_rows), BF16), "low": pltpu.VMEM((basis, local_rows), BF16),
        "blocks": pltpu.VMEM(tiles.shape, F32),
        "left": pltpu.VMEM((local_rows // PART, PART, LANES), BF16),
        "right": pltpu.VMEM((local_rows // PART, PART, LANES), BF16),
        "even": pltpu.VMEM((local_rows // 4, LANES), F32), "odd": pltpu.VMEM((local_rows // 4, LANES), F32),
        "faces": pltpu.VMEM((ROUNDS, width, face_rows), F32),
        "edge": pltpu.VMEM((2, width, LANES), F32),
        "match": pltpu.VMEM((ROUNDS, face_rows), jnp.int32), "weight": pltpu.VMEM((ROUNDS, face_rows), F32),
        "diag": pltpu.VMEM((1, local_rows), F32),
        "src": pltpu.VMEM(tiled, jnp.int32), "dest": pltpu.VMEM(tiled, jnp.int32),
        "tgt": pltpu.VMEM(tiled, jnp.int32), "w": pltpu.VMEM(tiled, F32),
        "index": pltpu.VMEM((slabs, LANES), jnp.int32), "index_smem": pltpu.SMEM((slabs, LANES), jnp.int32),
        "wet_rows": pltpu.VMEM((local_rows, LANES), F32),
        "pack": slab, "got": slab,
        "acc": pltpu.VMEM((bands, 2 * LANES), F32),
        "g_stage": cross_piece, "g_slots": cross_piece, "g_total": cross_piece,
        "g_along": pltpu.VMEM((dev, basis // plane, basis), F32),
        "h_stage": head_piece, "h_slots": head_piece, "h_total": head_piece,
        "h_along": pltpu.VMEM((dev, width // plane, lanes), F32),
        "local_sems": dma((7,)), "held_sems": dma((2,)), "block_sems": dma((group,)),
        "face_sems": dma((2, ROUNDS)), "edge_sems": dma((2, 2)), "twin_sems": dma((2,)),
        "wet_sems": dma((2, subdomains)), "g_sems": dma((6,)), "h_sems": dma((6,)),
    }
    names = (*inputs, *outputs, *scratch)
    next_block, coef, factor = pl.pallas_call(
        functools.partial(step_kernel, names, subdomains, used, total_rows),
        out_shape=tuple(outputs.values()),
        in_specs=[any_spec] * len(inputs),
        out_specs=(spec,) * len(outputs),
        scratch_shapes=list(scratch.values()),
        compiler_params=pltpu.CompilerParams(
            vmem_limit_bytes=52 << 20, collective_id=0, has_side_effects=True
        ),
    )(*(pltpu.with_memory_space_constraint(value, pltpu.HBM) for value in inputs.values()))
    return (next_block, coef.reshape(prior.shape[0], width, width), factor)


def solution(mesh):
    placed = (
        P(None, ALL),
        P(None, None, ALL),
        P(("grp", "dev"), None, None),
        P(("grp", "dev"), None),
        P(("grp", "dev"), None, None),
        P(("grp", "dev"), None, None),
        P(("grp", "dev")),
        P(("grp", "dev")),
        P(("grp", "dev"), None),
        P(("grp", "dev")),
        P(("grp", "dev")),
    )
    return jax.shard_map(
        shards, mesh=mesh, in_specs=placed, out_specs=(P(None, ALL), P(), P()), check_vma=False
    )
```

```python
import functools

import jax
import jax.numpy as jnp
from jax import lax
from jax.experimental import pallas as pl
from jax.experimental.pallas import tpu as pltpu
from jax.sharding import PartitionSpec as P

BS = 96
NB = 6
ROUNDS = 4
LANES = 128
QUAD = 4
PART = 32
F32 = jnp.float32
BF16 = jnp.bfloat16
NT = (((1,), (1,)), ((), ()))
ALL = ("sec", "grp", "dev")


def split2(x):
    hi = x.astype(BF16)
    return hi, (x - hi.astype(F32)).astype(BF16)


def nt(a, b):
    return lax.dot_general(a, b, NT, preferred_element_type=F32)


def lane_gather(x, low):
    return jnp.take_along_axis(x, low, axis=1)


def wet_sort(subdomains, limit, src_ref, dest_ref, tgt_ref, w_ref, index_ref, pack_ref):
    blocks = src_ref.shape[0]
    slabs = subdomains * QUAD
    top = pack_ref.shape[1] - 2 * QUAD
    dest = dest_ref[...]
    lane = lax.broadcasted_iota(jnp.int32, (LANES, LANES), 1)
    sub = lax.broadcasted_iota(jnp.int32, (LANES, LANES), 0)
    tri = jnp.where(sub < lane, 1.0, 0.0).astype(BF16)
    ones = jnp.ones((LANES, LANES), BF16)
    low_tri = jnp.where(
        lax.broadcasted_iota(jnp.int32, (blocks, blocks), 1)
        < lax.broadcasted_iota(jnp.int32, (blocks, blocks), 0),
        1.0,
        0.0,
    ).astype(BF16)

    def count(q, rank):
        mine = dest == q
        oh = jnp.where(mine, 1.0, 0.0).astype(BF16)
        within = jnp.dot(oh, tri, preferred_element_type=F32)
        totals = jnp.dot(oh, ones, preferred_element_type=F32).astype(BF16)
        offset = jnp.dot(low_tri, totals, preferred_element_type=F32)
        return jnp.where(mine, within + offset, rank)

    rank = lax.fori_loop(0, subdomains, count, jnp.zeros(dest.shape, F32)).astype(jnp.int32)
    slab = dest * QUAD + rank % QUAD
    spot = rank // QUAD
    src = src_ref[...]
    tgt = tgt_ref[...]
    w = w_ref[...]
    w0 = w.astype(BF16).astype(F32)
    w1 = (w - w0).astype(BF16).astype(F32)
    w2 = w - w0 - w1
    fields = [src // LANES, src % LANES, tgt // LANES, tgt % LANES]
    fields = [f.astype(F32) for f in fields] + [w0, w1, w2]
    acc = jnp.zeros((len(fields) * slabs, LANES), F32)
    slab_row = lax.broadcasted_iota(jnp.int32, (slabs, LANES), 0)
    for i in range(blocks):
        hit = slab_row == slab[i : i + 1, :]
        lhs = jnp.concatenate([jnp.where(hit, f[i : i + 1, :], 0.0) for f in fields], axis=0)
        oh = jnp.where(sub == spot[i : i + 1, :], 1.0, 0.0)
        acc = acc + nt(lhs.astype(BF16), oh.astype(BF16))
    parts = [acc[f * slabs : (f + 1) * slabs] for f in range(len(fields))]
    index = (parts[0] * LANES + parts[1]).astype(jnp.int32)
    index = jnp.minimum(jnp.maximum(index, 0), limit - 1)
    target = parts[2] * LANES + parts[3]
    weight = parts[4] + parts[5] + parts[6]
    for q in range(subdomains):
        index_ref[q] = index[q * QUAD : (q + 1) * QUAD]
        pack_ref[q, top - 8 : top] = jnp.zeros((8, LANES), F32)
        pack_ref[q, top : top + QUAD] = target[q * QUAD : (q + 1) * QUAD]
        pack_ref[q, top + QUAD :] = weight[q * QUAD : (q + 1) * QUAD]


class Wet:
    def __init__(
        self, subdomains, used, mine, x_ref, rows_ref, index_ref, index_smem, index_sems, pack_ref, got_ref,
        acc_ref, sems,
    ):
        self.used, self.index_smem, self.index_sems = used, index_smem, index_sems
        self.subdomains, self.mine, self.x_ref, self.rows_ref = subdomains, mine, x_ref, rows_ref
        self.index_ref, self.pack_ref, self.got_ref, self.acc_ref, self.sems = index_ref, pack_ref, got_ref, acc_ref, sems
        self.width, self.rows = x_ref.shape
        self.top = pack_ref.shape[1] - 2 * QUAD

    def prepare(self, first, last):
        def body(t, carry):
            at = pl.ds(pl.multiple_of(t * LANES, LANES), LANES)
            self.rows_ref[at, :] = jnp.concatenate([self.x_ref[:, at]] * QUAD, axis=0).T
            return carry

        lax.fori_loop(first, last, body, 0, unroll=4)

    def gather(self, b, q):
        lane = lax.broadcasted_iota(jnp.int32, (1, LANES), 1)
        masks = [lane < LANES * (g + 1) // QUAD for g in range(QUAD - 1)]
        for row in range(self.used):
            line = [self.rows_ref[self.index_smem[b, g, row]][None, :] for g in range(QUAD)]
            got = line[-1]
            for g in reversed(range(QUAD - 1)):
                got = jnp.where(masks[g], line[g], got)
            self.pack_ref[q, row : row + 1, :] = got

    def index_copy(self, b, s):
        q = lax.rem(self.mine + s, self.subdomains)
        return pltpu.make_async_copy(self.index_ref.at[q], self.index_smem.at[b], self.index_sems.at[b])

    def copy(self, to, at):
        return remote(
            self.pack_ref.at[to], self.got_ref.at[at], self.sems.at[0, to],
            self.sems.at[1, at], place(self.subdomains + to),
        )

    def send(self):
        def body(t, carry):
            for b in range(2):
                s = 2 * t + 1 + b
                q = lax.rem(self.mine + s, self.subdomains)
                self.index_copy(b, s).wait()
                self.gather(b, q)
                self.index_copy(b, s + 2).start()

                @pl.when(s < self.subdomains)
                def _():
                    self.copy(q, self.mine).start()

            return carry

        lax.fori_loop(0, self.subdomains // 2, body, 0)
        for b in range(2):
            self.index_copy(b, self.subdomains + 1 + b).wait()

    def add(self, sources, first):
        width, wide, top = self.width, 2 * LANES, self.top
        highs = self.rows // wide
        pad = jnp.zeros((LANES - top - 2 * QUAD, LANES), F32)
        subs = lax.broadcasted_iota(jnp.int32, (wide, LANES), 0).astype(F32).astype(BF16)
        one, zero = jnp.ones((wide, LANES), BF16), jnp.zeros((wide, LANES), BF16)
        none = jnp.zeros((width, LANES), BF16)
        terms, high, ohs = [], [], []
        for ref, q in sources:
            turned = jnp.concatenate([ref[q], pad], axis=0).T
            for g in range(QUAD):
                target = ref[q, top + g : top + g + 1].astype(jnp.int32)
                vals = turned[g * width : (g + 1) * width] * ref[q, top + QUAD + g : top + QUAD + g + 1]
                terms.append(split2(vals))
                high.append(jnp.broadcast_to((target // wide).astype(F32), (width, LANES)).astype(BF16))
                low = jnp.broadcast_to((target % wide).astype(F32), (wide, LANES)).astype(BF16)
                oh = jnp.where(subs == low, one, zero)
                ohs += [oh, oh]
        bands = []
        for h in range(highs):
            level = jnp.full((width, LANES), h, F32).astype(BF16)
            bands.append(
                jnp.concatenate([jnp.where(up == level, t, none) for up, two in zip(high, terms) for t in two], axis=1)
            )
        more = nt(jnp.concatenate(bands, axis=0), jnp.concatenate(ohs, axis=1))
        if first:
            self.acc_ref[...] = more
        else:
            self.acc_ref[...] += more

    def receive(self, first, last):
        subdomains, mine = self.subdomains, self.mine

        def arrived(s):
            q = lax.rem(mine + subdomains - s, subdomains)
            self.copy(q, q).wait_recv()
            return self.got_ref, q

        def take(s, carry):
            self.add([arrived(2 * s), arrived(2 * s + 1)], False)
            return carry

        if first == 0:
            self.add([(self.pack_ref, mine), arrived(1)], True)
        lax.fori_loop(max(first, 1), last, take, 0)

    def drain(self):
        def body(s, carry):
            self.copy(lax.rem(self.mine + s, self.subdomains), self.mine).wait_send()
            return carry

        lax.fori_loop(1, self.subdomains, body, 0)


def fluid_image(mine, subdomains, own_ref, diag_ref, edge_ref, acc_ref, image_ref):
    width, rows = own_ref.shape
    edges = [
        jnp.where(mine == 0, 0.0, edge_ref[0]),
        jnp.where(mine == subdomains - 1, 0.0, edge_ref[1]),
    ]
    lane = lax.broadcasted_iota(jnp.int32, (width, LANES), 1)
    pieces = rows // LANES
    for t in range(pieces):
        own = own_ref[:, t * LANES : (t + 1) * LANES]
        prev = edges[0] if t == 0 else own_ref[:, (t - 1) * LANES : t * LANES]
        nxt = edges[1] if t == pieces - 1 else own_ref[:, (t + 1) * LANES : (t + 2) * LANES]
        before = jnp.where(lane == 0, pltpu.roll(prev, 1, 1), pltpu.roll(own, 1, 1))
        after = jnp.where(
            lane == LANES - 1, pltpu.roll(nxt, LANES - 1, 1), pltpu.roll(own, LANES - 1, 1)
        )
        h, side = t // 2, t % 2
        added = acc_ref[h * width : (h + 1) * width, side * LANES : (side + 1) * LANES]
        d = diag_ref[:, t * LANES : (t + 1) * LANES]
        image_ref[:, t * LANES : (t + 1) * LANES] = d * own - before - after + added


def stack_terms(hi, lo):
    zero = jnp.zeros_like(hi)
    return jnp.concatenate([hi, lo, zero, zero, zero, zero, hi, lo], axis=0)


def shell_prepare(x_ref, left_ref, right_ref):
    lanes = lax.broadcasted_iota(jnp.int32, (LANES, LANES), 1)
    subs = lax.broadcasted_iota(jnp.int32, (LANES, LANES), 0)
    eye = jnp.where(lanes == subs, 1.0, 0.0).astype(BF16)

    def body(t, carry):
        at = pl.ds(pl.multiple_of(t * LANES, LANES), LANES)
        v = x_ref[:, at]
        hi = v.astype(BF16).astype(F32)
        both = nt(eye, stack_terms(hi, v - hi).astype(BF16)).astype(BF16)
        to = pl.ds(t * (LANES // PART), LANES // PART)
        left_ref[to] = both[:, :LANES].reshape(LANES // PART, PART, LANES)
        right_ref[to] = both[:, LANES:].reshape(LANES // PART, PART, LANES)
        return carry

    lax.fori_loop(0, x_ref.shape[1] // LANES, body, 0, unroll=4)


def shell_rows(group, cols_ref, blocks_ref, left_ref, right_ref, even_ref, odd_ref):
    chunks = BS * BS // LANES
    high = chunks // 3
    lane = lax.broadcasted_iota(jnp.int32, (high, LANES), 1)
    first = lane % (LANES // 2) < LANES // 4
    front = lane < LANES // 2
    for r in range(8):
        row = group * 8 + r
        at = [cols_ref[b, row] * (BS // PART) for b in range(NB)]
        outs = []
        for s in range(3):
            v = jnp.concatenate(
                [
                    blocks_ref[b, pl.ds(group * chunks * 8 + 8 * s + r, high, stride=24), :]
                    for b in range(NB)
                ],
                axis=1,
            )
            hi = v.astype(BF16).astype(F32)
            lhs = jnp.concatenate([hi, v - hi], axis=0).astype(BF16)
            spans = (
                ((left_ref, 0), (left_ref, 1), (left_ref, 2), (right_ref, 0)),
                ((right_ref, 1), (right_ref, 2), (left_ref, 0), (left_ref, 1)),
                ((left_ref, 2), (right_ref, 0), (right_ref, 1), (right_ref, 2)),
            )[s]
            rhs = jnp.concatenate([ref[at[b] + o] for b in range(NB) for ref, o in spans], axis=0)
            outs.append(jnp.dot(lhs, rhs, preferred_element_type=F32))

        def fold(z):
            return z[:high] + jnp.where(first, z[high:], 0.0)

        u = [fold(z) for z in outs]
        to = pl.ds(pl.multiple_of(row * high, 8), high)
        even_ref[to, :] = u[0] + jnp.where(front, 0.0, u[1])
        odd_ref[to, :] = u[2] + jnp.where(front, u[1], 0.0)


def shell_store(even_ref, odd_ref, out_ref):
    width = out_ref.shape[0]
    lane = lax.broadcasted_iota(jnp.int32, (width, LANES), 1)
    phase = lane % 4

    def body(t, carry):
        at = pl.ds(pl.multiple_of(t * LANES, LANES), LANES)
        even, odd = even_ref[at, :].T, odd_ref[at, :].T
        y = [
            even[:width] + even[width : 2 * width],
            even[2 * width : 3 * width] + even[3 * width :],
            odd[:width] + odd[width : 2 * width],
            odd[2 * width : 3 * width] + odd[3 * width :],
        ]
        for o in range(4):
            index = lane // 4 + 32 * o
            g = [lane_gather(v, index) for v in y]
            got = jnp.where(phase == 0, g[0], jnp.where(phase == 1, g[1], jnp.where(phase == 2, g[2], g[3])))
            out_ref[:, pl.ds(pl.multiple_of(t * 4 * LANES, LANES) + o * LANES, LANES)] = got
        return carry

    lax.fori_loop(0, even_ref.shape[0] // LANES, body, 0)


def add_faces(faces_ref, match_ref, weight_ref, out_ref):
    width = out_ref.shape[0]
    rounds, face = match_ref.shape
    pieces = face // LANES
    for m in range(rounds):
        for o in range(pieces):
            index = match_ref[m : m + 1, o * LANES : (o + 1) * LANES]
            high = jnp.broadcast_to(index // LANES, (width, LANES))
            low = jnp.broadcast_to(index % LANES, (width, LANES))
            got = jnp.zeros((width, LANES), F32)
            for h in range(pieces):
                piece = lane_gather(faces_ref[m, :, h * LANES : (h + 1) * LANES], low)
                got = jnp.where(high == h, piece, got)
            at = m * face + o * LANES
            w = weight_ref[m : m + 1, o * LANES : (o + 1) * LANES]
            out_ref[:, at : at + LANES] += w * got


MESH = pl.DeviceIdType.MESH


def place(index):
    dev = lax.axis_size("dev")
    grp = lax.axis_size("grp")
    return (index // (grp * dev), index // dev % grp, index % dev)


def turns(axis):
    count = lax.axis_size(axis)
    ring = [lax.axis_index(axis)]
    for _ in range(1, count):
        following = ring[-1] + 1
        ring.append(jnp.where(following == count, 0, following))
    return ring


def announce():
    barrier = pltpu.get_barrier_semaphore()
    rings = [turns(axis) for axis in ALL]
    for i, s in enumerate(rings[0]):
        for j, g in enumerate(rings[1]):
            for k, d in enumerate(rings[2]):
                if i or j or k:
                    pl.semaphore_signal(barrier, inc=1, device_id=(s, g, d), device_id_type=MESH)
    return barrier


def remote(src, dst, send, recv, device):
    return pltpu.make_async_remote_copy(
        src_ref=src, dst_ref=dst, send_sem=send, recv_sem=recv, device_id=device,
        device_id_type=MESH,
    )


class Reduce:
    def __init__(self, stage, slots, along, total, sems):
        self.stage, self.slots, self.along, self.total, self.sems = stage, slots, along, total, sems
        self.sec, self.g, self.d = (lax.axis_index(axis) for axis in ALL)
        self.grp = lax.axis_size("grp")
        self.me = self.sec * self.grp + self.g

    def plane(self, body):
        for i, s in enumerate(turns("sec")):
            for j, g in enumerate(turns("grp")):
                if i or j:
                    body(s * self.grp + g, (s, g, self.d))

    def bulk(self, source, target, first):
        rest = pl.ds(0, source.shape[0] - 1)
        other = (1 - self.sec, self.g, self.d)
        return remote(source.at[rest], target.at[rest], self.sems.at[first], self.sems.at[first + 1], other)

    def scatter(self):
        self.plane(
            lambda p, where: remote(
                self.stage.at[p], self.slots.at[self.me], self.sems.at[0], self.sems.at[1], where
            ).start()
        )

    def middle(self):
        self.bulk(self.stage, self.slots, 0).wait_recv()
        self.slots[self.me] = self.stage[self.me]
        self.along[self.d] = jnp.sum(self.slots[...], axis=0)
        for d in turns("dev")[1:]:
            remote(
                self.along.at[self.d], self.along.at[self.d], self.sems.at[2], self.sems.at[3],
                (self.sec, self.g, d),
            ).start()

    def gather(self):
        self.bulk(self.along, self.along, 2).wait_recv()
        self.total[self.me] = jnp.sum(self.along[...], axis=0)
        self.plane(
            lambda p, where: remote(
                self.total.at[self.me], self.total.at[self.me], self.sems.at[4], self.sems.at[5], where
            ).start()
        )

    def finish(self):
        self.bulk(self.total, self.total, 4).wait_recv()

    def drain(self):
        self.bulk(self.stage, self.slots, 0).wait_send()
        self.bulk(self.along, self.along, 2).wait_send()
        self.bulk(self.total, self.total, 4).wait_send()


def step_kernel(names, subdomains, used, total_rows, *refs):
    r = dict(zip(names, refs))
    n = 2 * subdomains
    sec, g, d = (lax.axis_index(axis) for axis in ALL)
    mine = g * lax.axis_size("dev") + d
    x_ref, image_ref = r["x"], r["image"]
    width, rows = x_ref.shape
    face = r["match"].shape[1]
    held, high_ref, low_ref = r["held"], r["high"], r["low"]
    basis = held.shape[0]
    chunk = rows // r["held_sems"].shape[0]
    groups = r["block_sems"].shape[0]

    def local(name, i):
        return pltpu.make_async_copy(r[name + "_hbm"], r[name], r["local_sems"].at[i])

    def prior_copy(i):
        at = pl.ds(pl.multiple_of(i * chunk, chunk), chunk)
        return pltpu.make_async_copy(r["prior_hbm"].at[:, at], held.at[:, at], r["held_sems"].at[i])

    def block_copy(i):
        span = r["blocks_hbm"].shape[1] // groups
        at = pl.ds(pl.multiple_of(i * span, 8), span)
        return pltpu.make_async_copy(r["blocks_hbm"].at[:, at], r["blocks"].at[:, at], r["block_sems"].at[i])

    structure = ("match", "weight", "cols")
    fluid = ("src", "dest", "tgt", "w", "diag")
    local("x", 0).start()

    @pl.when(sec == 1)
    def _():
        for i, name in enumerate(fluid):
            local(name, 1 + i).start()

    for i in range(rows // chunk):
        prior_copy(i).start()

    @pl.when(sec == 0)
    def _():
        for i in range(groups):
            block_copy(i).start()
        for i, name in enumerate(structure):
            local(name, 1 + i).start()

    barrier = announce()
    wet = Wet(
        subdomains, used, mine, r["xs"], r["wet_rows"], r["index"], r["index_smem"], r["index_sems"], r["pack"], r["got"], r["acc"], r["wet_sems"]
    )
    local("x", 0).wait()

    @pl.when(sec == 0)
    def _():
        shell_prepare(x_ref, r["left"], r["right"])

    @pl.when(sec == 1)
    def _():
        for i, name in enumerate(fluid):
            local(name, 1 + i).wait()
        wet_sort(subdomains, rows, r["src"], r["dest"], r["tgt"], r["w"], r["index"], r["pack"])
        for b in range(2):
            wet.index_copy(b, 1 + b).start()

    pl.semaphore_wait(barrier, n - 1)
    partners = [
        (0, g, d + 1 - 2 * lax.rem(d, 2)),
        (0, g, d + 2 - 4 * lax.rem(d // 2, 2)),
        (0, g + 1 - 2 * lax.rem(g, 2), d),
        (0, g + 2 - 4 * lax.rem(g // 2, 2), d),
    ]

    def face_copy(m):
        return remote(
            x_ref.at[:, pl.ds(m * face, face)], r["faces"].at[m], r["face_sems"].at[0, m],
            r["face_sems"].at[1, m], partners[m],
        )

    def edge_copy(side):
        to = subdomains + lax.rem(mine + (1 if side == 0 else subdomains - 1), subdomains)
        at = rows - LANES if side == 0 else 0
        return remote(
            x_ref.at[:, pl.ds(at, LANES)], r["edge"].at[side], r["edge_sems"].at[0, side],
            r["edge_sems"].at[1, side], place(to),
        )

    def twin_copy(m):
        at = pl.ds(m * face, face)
        return remote(
            x_ref.at[:, at], r["xs"].at[:, at], r["twin_sems"].at[0, m], r["twin_sems"].at[1, m], (1, g, d)
        )

    @pl.when(sec == 0)
    def _():
        for m in range(ROUNDS):
            twin_copy(m).start()
        for m in range(ROUNDS):
            face_copy(m).start()

    @pl.when(sec == 1)
    def _():
        edge_copy(0).start()
        edge_copy(1).start()


    def shell(first, last):
        def body(i, carry):
            block_copy(i).wait()
            shell_rows(i, r["cols"], r["blocks"], r["left"], r["right"], r["even"], r["odd"])
            return carry

        lax.fori_loop(first, last, body, 0)

    @pl.when(sec == 0)
    def _():
        local("cols", 3).wait()
        shell(0, groups)

    @pl.when(sec == 1)
    def _():
        for m in range(ROUNDS):
            twin_copy(m).wait_recv()
            wet.prepare(m * face // LANES, (m + 1) * face // LANES)
        wet.send()

    def product(i, carry):
        same, mixed = carry
        prior_copy(i).wait()
        at = pl.ds(pl.multiple_of(i * chunk, chunk), chunk)
        hi, lo = split2(held[:, at])
        high_ref[:, at] = hi
        low_ref[:, at] = lo
        return same + nt(hi, hi), mixed + nt(hi, lo)

    zero = jnp.zeros((basis, basis), F32)
    same, mixed = lax.fori_loop(0, rows // chunk, product, (zero, zero))
    part = same + mixed + mixed.T
    cross_sum = Reduce(r["g_stage"], r["g_slots"], r["g_along"], r["g_total"], r["g_sems"])
    half = basis // 2
    part = jnp.concatenate([part[:half, :half], part[:half, half:], part[half:, half:]], axis=0)
    cross_sum.stage[...] = part.reshape(cross_sum.stage.shape)
    cross_sum.scatter()

    @pl.when(sec == 0)
    def _():
        shell_store(r["even"], r["odd"], image_ref)

    pairs = subdomains // 2

    @pl.when(sec == 1)
    def _():
        wet.receive(0, pairs // 2)

    cross_sum.middle()

    @pl.when(sec == 0)
    def _():
        for i, name in enumerate(structure[:2]):
            local(name, 1 + i).wait()
        for m in range(ROUNDS):
            face_copy(m).wait()
        add_faces(r["faces"], r["match"], r["weight"], image_ref)
        for m in range(ROUNDS):
            twin_copy(m).wait_send()

    @pl.when(sec == 1)
    def _():
        wet.receive(pairs // 2, pairs)
        edge_copy(0).wait()
        edge_copy(1).wait()
        fluid_image(mine, subdomains, x_ref, r["diag"], r["edge"], r["acc"], image_ref)
        wet.drain()

    cross_sum.gather()
    ih, il = split2(image_ref[...])
    both = nt(jnp.concatenate([ih, il], axis=0), high_ref[...])
    head = both[:width] + both[width:] + nt(ih, low_ref[...])
    mixed = nt(ih, il)
    square = nt(ih, ih) + mixed + mixed.T
    part = jnp.concatenate(
        [head, square, jnp.zeros((width, -(basis + width) % LANES), F32)], axis=1
    )
    head_sum = Reduce(r["h_stage"], r["h_slots"], r["h_along"], r["h_total"], r["h_sems"])
    count, piece = head_sum.stage.shape[:2]
    for i in range(count):
        head_sum.stage[i] = part[i * piece : (i + 1) * piece]
    head_sum.scatter()
    cross_sum.finish()
    cross_sum.drain()
    head_sum.middle()
    blocks = cross_sum.total[...].reshape(3 * half, half)
    corner = blocks[half : 2 * half]
    cross = jnp.concatenate(
        [
            jnp.concatenate([blocks[:half], corner], axis=1),
            jnp.concatenate([corner.T, blocks[2 * half :]], axis=1),
        ],
        axis=0,
    )
    highest = lax.Precision.HIGHEST

    def dot(a, b):
        return jnp.dot(a, b, precision=highest, preferred_element_type=F32)

    def dot_nt(a, b):
        return lax.dot_general(a, b, NT, precision=highest, preferred_element_type=F32)

    eye = jnp.where(
        lax.broadcasted_iota(jnp.int32, (basis, basis), 0) == lax.broadcasted_iota(jnp.int32, (basis, basis), 1),
        1.0,
        0.0,
    )
    twice = 2.0 * eye - cross
    r["twice"][...] = twice
    r["drop"][...] = 2.0 * twice - dot(twice, dot(cross, twice))
    head_sum.gather()
    head_sum.finish()
    head_sum.drain()
    summed = jnp.concatenate([head_sum.total[i] for i in range(count)], axis=0)
    first = summed[:, :basis]
    square = summed[:, basis : basis + width]
    coef = dot(first, r["twice"][...])
    gram = (square - dot_nt(dot(first, r["drop"][...]), first)) * (1.0 / total_rows)
    r["coef"][...] = coef.T
    sub = lax.broadcasted_iota(jnp.int32, (width, 2 * width), 0)
    lane = lax.broadcasted_iota(jnp.int32, (width, 2 * width), 1)
    eye = jnp.where(sub + width == lane, 1.0, 0.0)
    work = jnp.concatenate([gram, jnp.zeros((width, width), F32)], axis=1) + eye
    for j in range(width):
        row = work[j : j + 1, :] / work[j : j + 1, j : j + 1]
        work = jnp.where(sub > j, work - work[:, j : j + 1] * row, work)
    pivots = jnp.sum(jnp.where(sub == lane, work, 0.0), axis=1, keepdims=True)
    work = work / jnp.sqrt(pivots)
    r["fac"][...] = jnp.where(sub <= lane, work, 0.0)[:, :width]
    inverse = work[:, width:]
    mix = -dot(inverse, coef)
    vh, vl = split2(inverse)
    mh, ml = split2(mix)
    vs = jnp.concatenate([vh, vl], axis=0)
    ms = jnp.concatenate([mh, ml], axis=0)

    def out(i, carry):
        at = pl.ds(pl.multiple_of(i * chunk, chunk), chunk)
        ih, il = split2(image_ref[:, at])
        a = jnp.dot(ms, high_ref[:, at], preferred_element_type=F32)
        a = a + jnp.dot(vs, ih, preferred_element_type=F32)
        c = jnp.dot(mh, low_ref[:, at], preferred_element_type=F32)
        c = c + jnp.dot(vh, il, preferred_element_type=F32)
        r["next"][:, at] = a[:width] + a[width:] + c
        return carry

    lax.fori_loop(0, rows // chunk, out, 0)


def settle_kernel(*refs):
    count = (len(refs) - 1) // 2
    copies = [pltpu.make_async_copy(refs[i], refs[count + i], refs[-1].at[i]) for i in range(count)]
    for copy in copies:
        copy.start()
    for copy in copies:
        copy.wait()


def shards(
    current, prior, block_values, block_cols, face_match, face_weight,
    fluid_diag, wet_source, wet_dest, wet_target, wet_weight,
):
    width, local_rows = current.shape
    face_rows = face_match.shape[2]
    row_blocks = block_cols.shape[0]
    wet_slots = wet_source.shape[0]
    grp, dev = lax.axis_size("grp"), lax.axis_size("dev")
    subdomains = grp * dev
    total_rows = local_rows * lax.axis_size("sec") * subdomains
    capacity = 2 * wet_slots // subdomains + 8
    slabs = subdomains * QUAD
    used = -(-capacity // QUAD)
    slots = -(-used // 8) * 8
    flat_prior = prior.reshape(-1, local_rows)
    basis = flat_prior.shape[0]
    plane = 2 * grp
    group = row_blocks // 8
    tiles = block_values.transpose(1, 0, 2).reshape(NB, group, 8, BS * BS // LANES, LANES)
    tiles = tiles.transpose(0, 1, 3, 2, 4).reshape(NB, row_blocks * BS * BS // LANES, LANES)
    tiled = (wet_slots // LANES, LANES)
    any_spec = pl.BlockSpec(memory_space=pl.ANY)
    spec = pl.BlockSpec(memory_space=pltpu.VMEM)
    inputs = {
        "x_hbm": current, "prior_hbm": flat_prior, "blocks_hbm": tiles, "cols_hbm": block_cols.T,
        "match_hbm": face_match[0], "weight_hbm": face_weight[0], "diag_hbm": fluid_diag[None, :],
        "src_hbm": wet_source.reshape(tiled), "dest_hbm": wet_dest.reshape(tiled),
        "tgt_hbm": wet_target.reshape(tiled), "w_hbm": wet_weight.reshape(tiled),
    }
    outputs = {
        "next": jax.ShapeDtypeStruct((width, local_rows), F32),
        "coef": jax.ShapeDtypeStruct((basis, width), F32),
        "fac": jax.ShapeDtypeStruct((width, width), F32),
    }
    lanes = -(-(basis + width) // LANES) * LANES
    slab = pltpu.VMEM((subdomains, slots + 2 * QUAD, LANES), F32)
    bands = local_rows // (2 * LANES) * width
    field = pltpu.VMEM((width, local_rows), F32)
    cross_piece = pltpu.VMEM((plane, 3 * basis // 2 // plane, basis // 2), F32)
    head_piece = pltpu.VMEM((plane, width // plane, lanes), F32)
    dma = pltpu.SemaphoreType.DMA
    scratch = {
        "cols": pltpu.SMEM((NB, row_blocks), jnp.int32),
        "image": field, "x": field, "xs": field,
        "held": pltpu.VMEM((basis, local_rows), F32),
        "high": pltpu.VMEM((basis, local_rows), BF16), "low": pltpu.VMEM((basis, local_rows), BF16),
        "blocks": pltpu.VMEM((NB, tiles.shape[1] + 32, LANES), F32),
        "left": pltpu.VMEM((local_rows // PART, PART, LANES), BF16),
        "right": pltpu.VMEM((local_rows // PART, PART, LANES), BF16),
        "even": pltpu.VMEM((local_rows // 4, LANES), F32), "odd": pltpu.VMEM((local_rows // 4, LANES), F32),
        "faces": pltpu.VMEM((ROUNDS, width, face_rows), F32),
        "edge": pltpu.VMEM((2, width, LANES), F32),
        "match": pltpu.VMEM((ROUNDS, face_rows), jnp.int32), "weight": pltpu.VMEM((ROUNDS, face_rows), F32),
        "diag": pltpu.VMEM((1, local_rows), F32),
        "src": pltpu.VMEM(tiled, jnp.int32), "dest": pltpu.VMEM(tiled, jnp.int32),
        "tgt": pltpu.VMEM(tiled, jnp.int32), "w": pltpu.VMEM(tiled, F32),
        "index": pltpu.VMEM((subdomains, QUAD, LANES), jnp.int32),
        "index_smem": pltpu.SMEM((2, QUAD, LANES), jnp.int32), "index_sems": dma((2,)),
        "wet_rows": pltpu.VMEM((local_rows, LANES), F32),
        "pack": slab, "got": slab,
        "acc": pltpu.VMEM((bands, 2 * LANES), F32),
        "g_stage": cross_piece, "g_slots": cross_piece, "g_total": cross_piece,
        "g_along": pltpu.VMEM((dev, 3 * basis // 2 // plane, basis // 2), F32),
        "twice": pltpu.VMEM((basis, basis), F32), "drop": pltpu.VMEM((basis, basis), F32),
        "h_stage": head_piece, "h_slots": head_piece, "h_total": head_piece,
        "h_along": pltpu.VMEM((dev, width // plane, lanes), F32),
        "local_sems": dma((6,)), "held_sems": dma((2,)), "block_sems": dma((group,)),
        "face_sems": dma((2, ROUNDS)), "edge_sems": dma((2, 2)), "twin_sems": dma((2, ROUNDS)),
        "wet_sems": dma((2, subdomains)), "g_sems": dma((6,)), "h_sems": dma((6,)),
    }
    names = (*inputs, *outputs, *scratch)
    next_block, coef, factor = pl.pallas_call(
        functools.partial(step_kernel, names, subdomains, used, total_rows),
        out_shape=tuple(outputs.values()),
        in_specs=[any_spec] * len(inputs),
        out_specs=(spec,) * len(outputs),
        scratch_shapes=list(scratch.values()),
        compiler_params=pltpu.CompilerParams(
            vmem_limit_bytes=52 << 20, collective_id=0, has_side_effects=True
        ),
    )(*(pltpu.with_memory_space_constraint(value, pltpu.HBM) for value in inputs.values()))
    next_block, coef, factor = pl.pallas_call(
        settle_kernel,
        out_shape=tuple(outputs.values()),
        in_specs=[spec] * len(outputs),
        out_specs=(any_spec,) * len(outputs),
        scratch_shapes=[dma((len(outputs),))],
        compiler_params=pltpu.CompilerParams(vmem_limit_bytes=8 << 20),
    )(next_block, coef, factor)
    return (next_block, coef.reshape(prior.shape[0], width, width), factor)


def solution(mesh):
    placed = (
        P(None, ALL),
        P(None, None, ALL),
        P(("grp", "dev"), None, None),
        P(("grp", "dev"), None),
        P(("grp", "dev"), None, None),
        P(("grp", "dev"), None, None),
        P(("grp", "dev")),
        P(("grp", "dev")),
        P(("grp", "dev"), None),
        P(("grp", "dev")),
        P(("grp", "dev")),
    )
    return jax.shard_map(
        shards, mesh=mesh, in_specs=placed, out_specs=(P(None, ALL), P(), P()), check_vma=False
    )
```

```python
import functools

import jax
import jax.numpy as jnp
from jax import lax
from jax.experimental import pallas as pl
from jax.experimental.pallas import tpu as pltpu
from jax.sharding import PartitionSpec as P

BS = 96
NB = 6
ROUNDS = 4
LANES = 128
QUAD = 4
PART = 32
F32 = jnp.float32
BF16 = jnp.bfloat16
NT = (((1,), (1,)), ((), ()))
ALL = ("sec", "grp", "dev")


def split2(x):
    hi = x.astype(BF16)
    return hi, (x - hi.astype(F32)).astype(BF16)


def nt(a, b):
    return lax.dot_general(a, b, NT, preferred_element_type=F32)


def lane_gather(x, low):
    return jnp.take_along_axis(x, low, axis=1)


def wet_sort(subdomains, limit, src_ref, dest_ref, tgt_ref, w_ref, index_ref, pack_ref):
    blocks = src_ref.shape[0]
    slabs = subdomains * QUAD
    top = pack_ref.shape[1] - 2 * QUAD
    dest = dest_ref[...]
    lane = lax.broadcasted_iota(jnp.int32, (LANES, LANES), 1)
    sub = lax.broadcasted_iota(jnp.int32, (LANES, LANES), 0)
    tri = jnp.where(sub < lane, 1.0, 0.0).astype(BF16)
    ones = jnp.ones((LANES, LANES), BF16)
    low_tri = jnp.where(
        lax.broadcasted_iota(jnp.int32, (blocks, blocks), 1)
        < lax.broadcasted_iota(jnp.int32, (blocks, blocks), 0),
        1.0,
        0.0,
    ).astype(BF16)

    def count(q, rank):
        mine = dest == q
        oh = jnp.where(mine, 1.0, 0.0).astype(BF16)
        within = jnp.dot(oh, tri, preferred_element_type=F32)
        totals = jnp.dot(oh, ones, preferred_element_type=F32).astype(BF16)
        offset = jnp.dot(low_tri, totals, preferred_element_type=F32)
        return jnp.where(mine, within + offset, rank)

    rank = lax.fori_loop(0, subdomains, count, jnp.zeros(dest.shape, F32)).astype(jnp.int32)
    slab = dest * QUAD + rank % QUAD
    spot = rank // QUAD
    src = src_ref[...]
    tgt = tgt_ref[...]
    w = w_ref[...]
    w0 = w.astype(BF16).astype(F32)
    w1 = (w - w0).astype(BF16).astype(F32)
    w2 = w - w0 - w1
    fields = [src // LANES, src % LANES, tgt // LANES, tgt % LANES]
    fields = [f.astype(F32) for f in fields] + [w0, w1, w2]
    acc = jnp.zeros((len(fields) * slabs, LANES), F32)
    slab_row = lax.broadcasted_iota(jnp.int32, (slabs, LANES), 0)
    for i in range(blocks):
        hit = slab_row == slab[i : i + 1, :]
        lhs = jnp.concatenate([jnp.where(hit, f[i : i + 1, :], 0.0) for f in fields], axis=0)
        oh = jnp.where(sub == spot[i : i + 1, :], 1.0, 0.0)
        acc = acc + nt(lhs.astype(BF16), oh.astype(BF16))
    parts = [acc[f * slabs : (f + 1) * slabs] for f in range(len(fields))]
    index = (parts[0] * LANES + parts[1]).astype(jnp.int32)
    index = jnp.minimum(jnp.maximum(index, 0), limit - 1)
    target = parts[2] * LANES + parts[3]
    weight = parts[4] + parts[5] + parts[6]
    for q in range(subdomains):
        index_ref[q] = index[q * QUAD : (q + 1) * QUAD]
        pack_ref[q, top - 8 : top] = jnp.zeros((8, LANES), F32)
        pack_ref[q, top : top + QUAD] = target[q * QUAD : (q + 1) * QUAD]
        pack_ref[q, top + QUAD :] = weight[q * QUAD : (q + 1) * QUAD]


class Wet:
    def __init__(
        self, subdomains, used, mine, x_ref, rows_ref, index_ref, index_smem, index_sems, pack_ref, got_ref,
        acc_ref, sems,
    ):
        self.used, self.index_smem, self.index_sems = used, index_smem, index_sems
        self.subdomains, self.mine, self.x_ref, self.rows_ref = subdomains, mine, x_ref, rows_ref
        self.index_ref, self.pack_ref, self.got_ref, self.acc_ref, self.sems = index_ref, pack_ref, got_ref, acc_ref, sems
        self.width, self.rows = x_ref.shape
        self.top = pack_ref.shape[1] - 2 * QUAD

    def prepare(self, first, last):
        def body(t, carry):
            at = pl.ds(pl.multiple_of(t * LANES, LANES), LANES)
            self.rows_ref[at, :] = jnp.concatenate([self.x_ref[:, at]] * QUAD, axis=0).T
            return carry

        lax.fori_loop(first, last, body, 0, unroll=4)

    def gather(self, b, q):
        lane = lax.broadcasted_iota(jnp.int32, (1, LANES), 1)
        masks = [lane < LANES * (g + 1) // QUAD for g in range(QUAD - 1)]
        for row in range(self.used):
            line = [self.rows_ref[self.index_smem[b, g, row]][None, :] for g in range(QUAD)]
            got = line[-1]
            for g in reversed(range(QUAD - 1)):
                got = jnp.where(masks[g], line[g], got)
            self.pack_ref[q, row : row + 1, :] = got

    def index_copy(self, b, s):
        q = lax.rem(self.mine + s, self.subdomains)
        return pltpu.make_async_copy(self.index_ref.at[q], self.index_smem.at[b], self.index_sems.at[b])

    def copy(self, to, at):
        return remote(
            self.pack_ref.at[to], self.got_ref.at[at], self.sems.at[0, to],
            self.sems.at[1, at], place(self.subdomains + to),
        )

    def send(self):
        def body(t, carry):
            for b in range(2):
                s = 2 * t + 1 + b
                q = lax.rem(self.mine + s, self.subdomains)
                self.index_copy(b, s).wait()
                self.gather(b, q)
                self.index_copy(b, s + 2).start()

                @pl.when(s < self.subdomains)
                def _():
                    self.copy(q, self.mine).start()

            return carry

        lax.fori_loop(0, self.subdomains // 2, body, 0)
        for b in range(2):
            self.index_copy(b, self.subdomains + 1 + b).wait()

    def add(self, sources, first):
        width, wide, top = self.width, 2 * LANES, self.top
        highs = self.rows // wide
        pad = jnp.zeros((LANES - top - 2 * QUAD, LANES), F32)
        subs = lax.broadcasted_iota(jnp.int32, (wide, LANES), 0).astype(F32).astype(BF16)
        one, zero = jnp.ones((wide, LANES), BF16), jnp.zeros((wide, LANES), BF16)
        none = jnp.zeros((width, LANES), BF16)
        terms, high, ohs = [], [], []
        for ref, q in sources:
            turned = jnp.concatenate([ref[q], pad], axis=0).T
            for g in range(QUAD):
                target = ref[q, top + g : top + g + 1].astype(jnp.int32)
                vals = turned[g * width : (g + 1) * width] * ref[q, top + QUAD + g : top + QUAD + g + 1]
                terms.append(split2(vals))
                high.append(jnp.broadcast_to((target // wide).astype(F32), (width, LANES)).astype(BF16))
                low = jnp.broadcast_to((target % wide).astype(F32), (wide, LANES)).astype(BF16)
                oh = jnp.where(subs == low, one, zero)
                ohs += [oh, oh]
        bands = []
        for h in range(highs):
            level = jnp.full((width, LANES), h, F32).astype(BF16)
            bands.append(
                jnp.concatenate([jnp.where(up == level, t, none) for up, two in zip(high, terms) for t in two], axis=1)
            )
        more = nt(jnp.concatenate(bands, axis=0), jnp.concatenate(ohs, axis=1))
        if first:
            self.acc_ref[...] = more
        else:
            self.acc_ref[...] += more

    def receive(self, first, last):
        subdomains, mine = self.subdomains, self.mine

        def arrived(s):
            q = lax.rem(mine + subdomains - s, subdomains)
            self.copy(q, q).wait_recv()
            return self.got_ref, q

        def take(s, carry):
            self.add([arrived(2 * s), arrived(2 * s + 1)], False)
            return carry

        if first == 0:
            self.add([(self.pack_ref, mine), arrived(1)], True)
        lax.fori_loop(max(first, 1), last, take, 0)

    def drain(self):
        def body(s, carry):
            self.copy(lax.rem(self.mine + s, self.subdomains), self.mine).wait_send()
            return carry

        lax.fori_loop(1, self.subdomains, body, 0)


def fluid_image(mine, subdomains, own_ref, diag_ref, edge_ref, acc_ref, image_ref):
    width, rows = own_ref.shape
    edges = [
        jnp.where(mine == 0, 0.0, edge_ref[0]),
        jnp.where(mine == subdomains - 1, 0.0, edge_ref[1]),
    ]
    lane = lax.broadcasted_iota(jnp.int32, (width, LANES), 1)
    pieces = rows // LANES
    for t in range(pieces):
        own = own_ref[:, t * LANES : (t + 1) * LANES]
        prev = edges[0] if t == 0 else own_ref[:, (t - 1) * LANES : t * LANES]
        nxt = edges[1] if t == pieces - 1 else own_ref[:, (t + 1) * LANES : (t + 2) * LANES]
        before = jnp.where(lane == 0, pltpu.roll(prev, 1, 1), pltpu.roll(own, 1, 1))
        after = jnp.where(
            lane == LANES - 1, pltpu.roll(nxt, LANES - 1, 1), pltpu.roll(own, LANES - 1, 1)
        )
        h, side = t // 2, t % 2
        added = acc_ref[h * width : (h + 1) * width, side * LANES : (side + 1) * LANES]
        d = diag_ref[:, t * LANES : (t + 1) * LANES]
        image_ref[:, t * LANES : (t + 1) * LANES] = d * own - before - after + added


def stack_terms(hi, lo):
    zero = jnp.zeros_like(hi)
    return jnp.concatenate([hi, lo, zero, zero, zero, zero, hi, lo], axis=0)


def shell_prepare(x_ref, left_ref, right_ref):
    lanes = lax.broadcasted_iota(jnp.int32, (LANES, LANES), 1)
    subs = lax.broadcasted_iota(jnp.int32, (LANES, LANES), 0)
    eye = jnp.where(lanes == subs, 1.0, 0.0).astype(BF16)

    def body(t, carry):
        at = pl.ds(pl.multiple_of(t * LANES, LANES), LANES)
        v = x_ref[:, at]
        hi = v.astype(BF16).astype(F32)
        both = nt(eye, stack_terms(hi, v - hi).astype(BF16)).astype(BF16)
        to = pl.ds(t * (LANES // PART), LANES // PART)
        left_ref[to] = both[:, :LANES].reshape(LANES // PART, PART, LANES)
        right_ref[to] = both[:, LANES:].reshape(LANES // PART, PART, LANES)
        return carry

    lax.fori_loop(0, x_ref.shape[1] // LANES, body, 0, unroll=4)


def shell_rows(group, cols_ref, blocks_ref, left_ref, right_ref, even_ref, odd_ref):
    chunks = BS * BS // LANES
    high = chunks // 3
    lane = lax.broadcasted_iota(jnp.int32, (high, LANES), 1)
    first = lane % (LANES // 2) < LANES // 4
    front = lane < LANES // 2
    for r in range(8):
        row = group * 8 + r
        at = [cols_ref[b, row] * (BS // PART) for b in range(NB)]
        outs = []
        for s in range(3):
            v = jnp.concatenate(
                [
                    blocks_ref[b, pl.ds(group * chunks * 8 + 8 * s + r, high, stride=24), :]
                    for b in range(NB)
                ],
                axis=1,
            )
            hi = v.astype(BF16).astype(F32)
            lhs = jnp.concatenate([hi, v - hi], axis=0).astype(BF16)
            spans = (
                ((left_ref, 0), (left_ref, 1), (left_ref, 2), (right_ref, 0)),
                ((right_ref, 1), (right_ref, 2), (left_ref, 0), (left_ref, 1)),
                ((left_ref, 2), (right_ref, 0), (right_ref, 1), (right_ref, 2)),
            )[s]
            rhs = jnp.concatenate([ref[at[b] + o] for b in range(NB) for ref, o in spans], axis=0)
            outs.append(jnp.dot(lhs, rhs, preferred_element_type=F32))

        def fold(z):
            return z[:high] + jnp.where(first, z[high:], 0.0)

        u = [fold(z) for z in outs]
        to = pl.ds(pl.multiple_of(row * high, 8), high)
        even_ref[to, :] = u[0] + jnp.where(front, 0.0, u[1])
        odd_ref[to, :] = u[2] + jnp.where(front, u[1], 0.0)


def shell_store(even_ref, odd_ref, out_ref):
    width = out_ref.shape[0]
    lane = lax.broadcasted_iota(jnp.int32, (width, LANES), 1)
    phase = lane % 4

    def body(t, carry):
        at = pl.ds(pl.multiple_of(t * LANES, LANES), LANES)
        even, odd = even_ref[at, :].T, odd_ref[at, :].T
        y = [
            even[:width] + even[width : 2 * width],
            even[2 * width : 3 * width] + even[3 * width :],
            odd[:width] + odd[width : 2 * width],
            odd[2 * width : 3 * width] + odd[3 * width :],
        ]
        for o in range(4):
            index = lane // 4 + 32 * o
            g = [lane_gather(v, index) for v in y]
            got = jnp.where(phase == 0, g[0], jnp.where(phase == 1, g[1], jnp.where(phase == 2, g[2], g[3])))
            out_ref[:, pl.ds(pl.multiple_of(t * 4 * LANES, LANES) + o * LANES, LANES)] = got
        return carry

    lax.fori_loop(0, even_ref.shape[0] // LANES, body, 0)


def add_faces(faces_ref, match_ref, weight_ref, out_ref):
    width = out_ref.shape[0]
    rounds, face = match_ref.shape
    pieces = face // LANES
    for m in range(rounds):
        for o in range(pieces):
            index = match_ref[m : m + 1, o * LANES : (o + 1) * LANES]
            high = jnp.broadcast_to(index // LANES, (width, LANES))
            low = jnp.broadcast_to(index % LANES, (width, LANES))
            got = jnp.zeros((width, LANES), F32)
            for h in range(pieces):
                piece = lane_gather(faces_ref[m, :, h * LANES : (h + 1) * LANES], low)
                got = jnp.where(high == h, piece, got)
            at = m * face + o * LANES
            w = weight_ref[m : m + 1, o * LANES : (o + 1) * LANES]
            out_ref[:, at : at + LANES] += w * got


MESH = pl.DeviceIdType.MESH


def place(index):
    dev = lax.axis_size("dev")
    grp = lax.axis_size("grp")
    return (index // (grp * dev), index // dev % grp, index % dev)


def turns(axis):
    count = lax.axis_size(axis)
    ring = [lax.axis_index(axis)]
    for _ in range(1, count):
        following = ring[-1] + 1
        ring.append(jnp.where(following == count, 0, following))
    return ring


def announce():
    barrier = pltpu.get_barrier_semaphore()
    rings = [turns(axis) for axis in ALL]
    for i, s in enumerate(rings[0]):
        for j, g in enumerate(rings[1]):
            for k, d in enumerate(rings[2]):
                if i or j or k:
                    pl.semaphore_signal(barrier, inc=1, device_id=(s, g, d), device_id_type=MESH)
    return barrier


def remote(src, dst, send, recv, device):
    return pltpu.make_async_remote_copy(
        src_ref=src, dst_ref=dst, send_sem=send, recv_sem=recv, device_id=device,
        device_id_type=MESH,
    )


class Reduce:
    def __init__(self, stage, slots, along, total, sems):
        self.stage, self.slots, self.along, self.total, self.sems = stage, slots, along, total, sems
        self.sec, self.g, self.d = (lax.axis_index(axis) for axis in ALL)
        self.grp = lax.axis_size("grp")
        self.me = self.sec * self.grp + self.g

    def plane(self, body):
        for i, s in enumerate(turns("sec")):
            for j, g in enumerate(turns("grp")):
                if i or j:
                    body(s * self.grp + g, (s, g, self.d))

    def bulk(self, source, target, first):
        rest = pl.ds(0, source.shape[0] - 1)
        other = (1 - self.sec, self.g, self.d)
        return remote(source.at[rest], target.at[rest], self.sems.at[first], self.sems.at[first + 1], other)

    def scatter(self):
        self.plane(
            lambda p, where: remote(
                self.stage.at[p], self.slots.at[self.me], self.sems.at[0], self.sems.at[1], where
            ).start()
        )

    def middle(self):
        self.bulk(self.stage, self.slots, 0).wait_recv()
        self.slots[self.me] = self.stage[self.me]
        self.along[self.d] = jnp.sum(self.slots[...], axis=0)
        for d in turns("dev")[1:]:
            remote(
                self.along.at[self.d], self.along.at[self.d], self.sems.at[2], self.sems.at[3],
                (self.sec, self.g, d),
            ).start()

    def gather(self):
        self.bulk(self.along, self.along, 2).wait_recv()
        self.total[self.me] = jnp.sum(self.along[...], axis=0)
        self.plane(
            lambda p, where: remote(
                self.total.at[self.me], self.total.at[self.me], self.sems.at[4], self.sems.at[5], where
            ).start()
        )

    def finish(self):
        self.bulk(self.total, self.total, 4).wait_recv()

    def drain(self):
        self.bulk(self.stage, self.slots, 0).wait_send()
        self.bulk(self.along, self.along, 2).wait_send()
        self.bulk(self.total, self.total, 4).wait_send()


def step_kernel(names, subdomains, used, total_rows, *refs):
    r = dict(zip(names, refs))
    n = 2 * subdomains
    sec, g, d = (lax.axis_index(axis) for axis in ALL)
    mine = g * lax.axis_size("dev") + d
    x_ref, image_ref = r["x"], r["image"]
    width, rows = x_ref.shape
    face = r["match"].shape[1]
    held, high_ref, low_ref = r["held"], r["high"], r["low"]
    basis = held.shape[0]
    chunk = rows // r["held_sems"].shape[0]
    groups = r["block_sems"].shape[0]

    def local(name, i):
        return pltpu.make_async_copy(r[name + "_hbm"], r[name], r["local_sems"].at[i])

    def prior_copy(i):
        at = pl.ds(pl.multiple_of(i * chunk, chunk), chunk)
        return pltpu.make_async_copy(r["prior_hbm"].at[:, at], held.at[:, at], r["held_sems"].at[i])

    def block_copy(i):
        span = r["blocks_hbm"].shape[1] // groups
        at = pl.ds(pl.multiple_of(i * span, 8), span)
        return pltpu.make_async_copy(r["blocks_hbm"].at[:, at], r["blocks"].at[:, at], r["block_sems"].at[i])

    structure = ("match", "weight", "cols")
    fluid = ("src", "dest", "tgt", "w", "diag")
    local("x", 0).start()

    @pl.when(sec == 1)
    def _():
        for i, name in enumerate(fluid):
            local(name, 1 + i).start()

    for i in range(rows // chunk):
        prior_copy(i).start()

    @pl.when(sec == 0)
    def _():
        for i in range(groups):
            block_copy(i).start()
        for i, name in enumerate(structure):
            local(name, 1 + i).start()

    barrier = announce()
    wet = Wet(
        subdomains, used, mine, r["xs"], r["wet_rows"], r["index"], r["index_smem"], r["index_sems"], r["pack"], r["got"], r["acc"], r["wet_sems"]
    )
    local("x", 0).wait()

    @pl.when(sec == 0)
    def _():
        shell_prepare(x_ref, r["left"], r["right"])

    @pl.when(sec == 1)
    def _():
        for i, name in enumerate(fluid):
            local(name, 1 + i).wait()
        wet_sort(subdomains, rows, r["src"], r["dest"], r["tgt"], r["w"], r["index"], r["pack"])
        for b in range(2):
            wet.index_copy(b, 1 + b).start()

    pl.semaphore_wait(barrier, n - 1)
    partners = [
        (0, g, d + 1 - 2 * lax.rem(d, 2)),
        (0, g, d + 2 - 4 * lax.rem(d // 2, 2)),
        (0, g + 1 - 2 * lax.rem(g, 2), d),
        (0, g + 2 - 4 * lax.rem(g // 2, 2), d),
    ]

    def face_copy(m):
        return remote(
            x_ref.at[:, pl.ds(m * face, face)], r["faces"].at[m], r["face_sems"].at[0, m],
            r["face_sems"].at[1, m], partners[m],
        )

    def edge_copy(side):
        to = subdomains + lax.rem(mine + (1 if side == 0 else subdomains - 1), subdomains)
        at = rows - LANES if side == 0 else 0
        return remote(
            x_ref.at[:, pl.ds(at, LANES)], r["edge"].at[side], r["edge_sems"].at[0, side],
            r["edge_sems"].at[1, side], place(to),
        )

    def twin_copy(m):
        at = pl.ds(m * face, face)
        return remote(
            x_ref.at[:, at], r["xs"].at[:, at], r["twin_sems"].at[0, m], r["twin_sems"].at[1, m], (1, g, d)
        )

    @pl.when(sec == 0)
    def _():
        for m in range(ROUNDS):
            twin_copy(m).start()
        for m in range(ROUNDS):
            face_copy(m).start()

    @pl.when(sec == 1)
    def _():
        edge_copy(0).start()
        edge_copy(1).start()


    def shell(first, last):
        def body(i, carry):
            block_copy(i).wait()
            shell_rows(i, r["cols"], r["blocks"], r["left"], r["right"], r["even"], r["odd"])
            return carry

        lax.fori_loop(first, last, body, 0)

    half = basis // 2
    cross_sum = Reduce(r["g_stage"], r["g_slots"], r["g_along"], r["g_total"], r["g_sems"])

    def cross_part():
        def product(i, carry):
            same, mixed = carry
            prior_copy(i).wait()
            at = pl.ds(pl.multiple_of(i * chunk, chunk), chunk)
            hi, lo = split2(held[:, at])
            high_ref[:, at] = hi
            low_ref[:, at] = lo
            return same + nt(hi, hi), mixed + nt(hi, lo)

        zero = jnp.zeros((basis, basis), F32)
        same, mixed = lax.fori_loop(0, rows // chunk, product, (zero, zero))
        part = same + mixed + mixed.T
        part = jnp.concatenate([part[:half, :half], part[:half, half:], part[half:, half:]], axis=0)
        cross_sum.stage[...] = part.reshape(cross_sum.stage.shape)
        cross_sum.scatter()

    @pl.when(sec == 0)
    def _():
        cross_part()
        local("cols", 3).wait()
        shell(0, groups)

    @pl.when(sec == 1)
    def _():
        for m in range(ROUNDS):
            twin_copy(m).wait_recv()
            wet.prepare(m * face // LANES, (m + 1) * face // LANES)
        wet.send()
        cross_part()


    @pl.when(sec == 0)
    def _():
        shell_store(r["even"], r["odd"], image_ref)

    pairs = subdomains // 2

    @pl.when(sec == 1)
    def _():
        wet.receive(0, pairs // 2)

    cross_sum.middle()

    @pl.when(sec == 0)
    def _():
        for i, name in enumerate(structure[:2]):
            local(name, 1 + i).wait()
        for m in range(ROUNDS):
            face_copy(m).wait()
        add_faces(r["faces"], r["match"], r["weight"], image_ref)
        for m in range(ROUNDS):
            twin_copy(m).wait_send()

    @pl.when(sec == 1)
    def _():
        wet.receive(pairs // 2, pairs)
    cross_sum.gather()

    @pl.when(sec == 1)
    def _():
        edge_copy(0).wait()
        edge_copy(1).wait()
        fluid_image(mine, subdomains, x_ref, r["diag"], r["edge"], r["acc"], image_ref)
        wet.drain()

    ih, il = split2(image_ref[...])
    both = nt(jnp.concatenate([ih, il], axis=0), high_ref[...])
    head = both[:width] + both[width:] + nt(ih, low_ref[...])
    mixed = nt(ih, il)
    square = nt(ih, ih) + mixed + mixed.T
    part = jnp.concatenate(
        [head, square, jnp.zeros((width, -(basis + width) % LANES), F32)], axis=1
    )
    head_sum = Reduce(r["h_stage"], r["h_slots"], r["h_along"], r["h_total"], r["h_sems"])
    count, piece = head_sum.stage.shape[:2]
    for i in range(count):
        head_sum.stage[i] = part[i * piece : (i + 1) * piece]
    head_sum.scatter()
    cross_sum.finish()
    cross_sum.drain()
    head_sum.middle()
    blocks = cross_sum.total[...].reshape(3 * half, half)
    corner = blocks[half : 2 * half]
    cross = jnp.concatenate(
        [
            jnp.concatenate([blocks[:half], corner], axis=1),
            jnp.concatenate([corner.T, blocks[2 * half :]], axis=1),
        ],
        axis=0,
    )
    highest = lax.Precision.HIGHEST

    def dot(a, b):
        return jnp.dot(a, b, precision=highest, preferred_element_type=F32)

    def dot_nt(a, b):
        return lax.dot_general(a, b, NT, precision=highest, preferred_element_type=F32)

    eye = jnp.where(
        lax.broadcasted_iota(jnp.int32, (basis, basis), 0) == lax.broadcasted_iota(jnp.int32, (basis, basis), 1),
        1.0,
        0.0,
    )
    twice = 2.0 * eye - cross
    r["twice"][...] = twice
    r["drop"][...] = 2.0 * twice - dot(twice, dot(cross, twice))
    head_sum.gather()
    head_sum.finish()
    head_sum.drain()
    summed = jnp.concatenate([head_sum.total[i] for i in range(count)], axis=0)
    first = summed[:, :basis]
    square = summed[:, basis : basis + width]
    coef = dot(first, r["twice"][...])
    gram = (square - dot_nt(dot(first, r["drop"][...]), first)) * (1.0 / total_rows)
    r["coef"][...] = coef.T
    sub = lax.broadcasted_iota(jnp.int32, (width, 2 * width), 0)
    lane = lax.broadcasted_iota(jnp.int32, (width, 2 * width), 1)
    eye = jnp.where(sub + width == lane, 1.0, 0.0)
    work = jnp.concatenate([gram, jnp.zeros((width, width), F32)], axis=1) + eye
    for j in range(width):
        row = work[j : j + 1, :] / work[j : j + 1, j : j + 1]
        work = jnp.where(sub > j, work - work[:, j : j + 1] * row, work)
    pivots = jnp.sum(jnp.where(sub == lane, work, 0.0), axis=1, keepdims=True)
    work = work / jnp.sqrt(pivots)
    r["fac"][...] = jnp.where(sub <= lane, work, 0.0)[:, :width]
    inverse = work[:, width:]
    mix = -dot(inverse, coef)
    vh, vl = split2(inverse)
    mh, ml = split2(mix)
    vs = jnp.concatenate([vh, vl], axis=0)
    ms = jnp.concatenate([mh, ml], axis=0)

    def out(i, carry):
        at = pl.ds(pl.multiple_of(i * chunk, chunk), chunk)
        ih, il = split2(image_ref[:, at])
        a = jnp.dot(ms, high_ref[:, at], preferred_element_type=F32)
        a = a + jnp.dot(vs, ih, preferred_element_type=F32)
        c = jnp.dot(mh, low_ref[:, at], preferred_element_type=F32)
        c = c + jnp.dot(vh, il, preferred_element_type=F32)
        r["next"][:, at] = a[:width] + a[width:] + c
        return carry

    lax.fori_loop(0, rows // chunk, out, 0)


def settle_kernel(*refs):
    count = (len(refs) - 1) // 2
    copies = [pltpu.make_async_copy(refs[i], refs[count + i], refs[-1].at[i]) for i in range(count)]
    for copy in copies:
        copy.start()
    for copy in copies:
        copy.wait()


def shards(
    current, prior, block_values, block_cols, face_match, face_weight,
    fluid_diag, wet_source, wet_dest, wet_target, wet_weight,
):
    width, local_rows = current.shape
    face_rows = face_match.shape[2]
    row_blocks = block_cols.shape[0]
    wet_slots = wet_source.shape[0]
    grp, dev = lax.axis_size("grp"), lax.axis_size("dev")
    subdomains = grp * dev
    total_rows = local_rows * lax.axis_size("sec") * subdomains
    capacity = 2 * wet_slots // subdomains + 8
    slabs = subdomains * QUAD
    used = -(-capacity // QUAD)
    slots = -(-used // 8) * 8
    flat_prior = prior.reshape(-1, local_rows)
    basis = flat_prior.shape[0]
    plane = 2 * grp
    group = row_blocks // 8
    tiles = block_values.transpose(1, 0, 2).reshape(NB, group, 8, BS * BS // LANES, LANES)
    tiles = tiles.transpose(0, 1, 3, 2, 4).reshape(NB, row_blocks * BS * BS // LANES, LANES)
    tiled = (wet_slots // LANES, LANES)
    any_spec = pl.BlockSpec(memory_space=pl.ANY)
    spec = pl.BlockSpec(memory_space=pltpu.VMEM)
    inputs = {
        "x_hbm": current, "prior_hbm": flat_prior, "blocks_hbm": tiles, "cols_hbm": block_cols.T,
        "match_hbm": face_match[0], "weight_hbm": face_weight[0], "diag_hbm": fluid_diag[None, :],
        "src_hbm": wet_source.reshape(tiled), "dest_hbm": wet_dest.reshape(tiled),
        "tgt_hbm": wet_target.reshape(tiled), "w_hbm": wet_weight.reshape(tiled),
    }
    outputs = {
        "next": jax.ShapeDtypeStruct((width, local_rows), F32),
        "coef": jax.ShapeDtypeStruct((basis, width), F32),
        "fac": jax.ShapeDtypeStruct((width, width), F32),
    }
    lanes = -(-(basis + width) // LANES) * LANES
    slab = pltpu.VMEM((subdomains, slots + 2 * QUAD, LANES), F32)
    bands = local_rows // (2 * LANES) * width
    field = pltpu.VMEM((width, local_rows), F32)
    cross_piece = pltpu.VMEM((plane, 3 * basis // 2 // plane, basis // 2), F32)
    head_piece = pltpu.VMEM((plane, width // plane, lanes), F32)
    dma = pltpu.SemaphoreType.DMA
    scratch = {
        "cols": pltpu.SMEM((NB, row_blocks), jnp.int32),
        "image": field, "x": field, "xs": field,
        "held": pltpu.VMEM((basis, local_rows), F32),
        "high": pltpu.VMEM((basis, local_rows), BF16), "low": pltpu.VMEM((basis, local_rows), BF16),
        "blocks": pltpu.VMEM((NB, tiles.shape[1] + 32, LANES), F32),
        "left": pltpu.VMEM((local_rows // PART, PART, LANES), BF16),
        "right": pltpu.VMEM((local_rows // PART, PART, LANES), BF16),
        "even": pltpu.VMEM((local_rows // 4, LANES), F32), "odd": pltpu.VMEM((local_rows // 4, LANES), F32),
        "faces": pltpu.VMEM((ROUNDS, width, face_rows), F32),
        "edge": pltpu.VMEM((2, width, LANES), F32),
        "match": pltpu.VMEM((ROUNDS, face_rows), jnp.int32), "weight": pltpu.VMEM((ROUNDS, face_rows), F32),
        "diag": pltpu.VMEM((1, local_rows), F32),
        "src": pltpu.VMEM(tiled, jnp.int32), "dest": pltpu.VMEM(tiled, jnp.int32),
        "tgt": pltpu.VMEM(tiled, jnp.int32), "w": pltpu.VMEM(tiled, F32),
        "index": pltpu.VMEM((subdomains, QUAD, LANES), jnp.int32),
        "index_smem": pltpu.SMEM((2, QUAD, LANES), jnp.int32), "index_sems": dma((2,)),
        "wet_rows": pltpu.VMEM((local_rows, LANES), F32),
        "pack": slab, "got": slab,
        "acc": pltpu.VMEM((bands, 2 * LANES), F32),
        "g_stage": cross_piece, "g_slots": cross_piece, "g_total": cross_piece,
        "g_along": pltpu.VMEM((dev, 3 * basis // 2 // plane, basis // 2), F32),
        "twice": pltpu.VMEM((basis, basis), F32), "drop": pltpu.VMEM((basis, basis), F32),
        "h_stage": head_piece, "h_slots": head_piece, "h_total": head_piece,
        "h_along": pltpu.VMEM((dev, width // plane, lanes), F32),
        "local_sems": dma((6,)), "held_sems": dma((2,)), "block_sems": dma((group,)),
        "face_sems": dma((2, ROUNDS)), "edge_sems": dma((2, 2)), "twin_sems": dma((2, ROUNDS)),
        "wet_sems": dma((2, subdomains)), "g_sems": dma((6,)), "h_sems": dma((6,)),
    }
    names = (*inputs, *outputs, *scratch)
    next_block, coef, factor = pl.pallas_call(
        functools.partial(step_kernel, names, subdomains, used, total_rows),
        out_shape=tuple(outputs.values()),
        in_specs=[any_spec] * len(inputs),
        out_specs=(spec,) * len(outputs),
        scratch_shapes=list(scratch.values()),
        compiler_params=pltpu.CompilerParams(
            vmem_limit_bytes=52 << 20, collective_id=0, has_side_effects=True
        ),
    )(*(pltpu.with_memory_space_constraint(value, pltpu.HBM) for value in inputs.values()))
    next_block, coef, factor = pl.pallas_call(
        settle_kernel,
        out_shape=tuple(outputs.values()),
        in_specs=[spec] * len(outputs),
        out_specs=(any_spec,) * len(outputs),
        scratch_shapes=[dma((len(outputs),))],
        compiler_params=pltpu.CompilerParams(vmem_limit_bytes=8 << 20),
    )(next_block, coef, factor)
    return (next_block, coef.reshape(prior.shape[0], width, width), factor)


def solution(mesh):
    placed = (
        P(None, ALL),
        P(None, None, ALL),
        P(("grp", "dev"), None, None),
        P(("grp", "dev"), None),
        P(("grp", "dev"), None, None),
        P(("grp", "dev"), None, None),
        P(("grp", "dev")),
        P(("grp", "dev")),
        P(("grp", "dev"), None),
        P(("grp", "dev")),
        P(("grp", "dev")),
    )
    return jax.shard_map(
        shards, mesh=mesh, in_specs=placed, out_specs=(P(None, ALL), P(), P()), check_vma=False
    )
```
